256 devices in a mesh: seq: 32 (over y, x, core), fsdp: 8 (over z).
Axes of the slice: x: 4, y: 4, z: 8, core: 2. Of those that a mesh axis runs over, the one named last changes fastest.
Arguments:
- queries: bfloat16 [8192, 3072], P('seq', 'fsdp'), may hold values from -64 to 64
- key_rows: bfloat16 [8192, 3072], P('seq', 'fsdp'), may hold values from -4 to 4
- value_rows: bfloat16 [8192, 3072], P('seq', 'fsdp'), may hold values from -6 to 6
- pattern: int32 [64, 8], P('seq'), may hold values from 0 to 63, as said below
- out_weight: bfloat16 [128, 24, 6144], P('seq', None, 'fsdp'), may hold values from -0.109375 to 0.109375
- out_grad: bfloat16 [8192, 6144], P('seq', 'fsdp'), may hold values from -6 to 6
Outputs:
- projected: bfloat16 [8192, 6144], P('seq', 'fsdp')
- query_grad: bfloat16 [8192, 3072], P('seq', 'fsdp')
- key_grad: bfloat16 [8192, 3072], P('seq', 'fsdp')
- value_grad: bfloat16 [8192, 3072], P('seq', 'fsdp')
- weight_grad: float32 [128, 24, 6144], P('seq', None, 'fsdp')
The draws below stay inside these ranges and needn't reach their ends.
Inputs may be any that keep to these rules, and one draw needn't show every extreme that they name: `pattern`: row i holds (i - 1) mod 64, i and (i + 1) mod 64 in columns 0 to 2; columns 3 and 4 hold the same two different blocks in every row; in columns 5 to 7, the 2 rows from any multiple of 2 name blocks of any one range o * 2 to (o + 1) * 2 - 1 at most 1 times together, and some range exactly 1 times.
All inputs are finite; a program needn't handle non-finite values.
Results may differ from the reference program's by a relative error of at most 0.035.
Values may be sent and summed in bfloat16 or wider, within the bound.
No kernel may reach another device: no remote copies, remote signals or barrier semaphores. Data moves between devices by JAX's collectives and lax.ppermute only.
A program may use at most 128 MiB of HBM per device.

```python
import math
import jax
import jax.numpy as jnp
from jax import lax

D = 6144
HEADS = 24
HD = 128
BLK = 128
NRAND = 3
QB_DEV = 2
NSEL = 8
NBLK = 64
TOKENS = 8192
N_SEQ = 32
N_FSDP = 8


def paired_draw(key):
    base_key = jax.random.fold_in(key, 71)
    first_key, second_key = jax.random.split(base_key)
    full_shape = (TOKENS, HEADS * HD)
    keys_out = jnp.clip(jax.random.normal(first_key, full_shape, jnp.float32), -4.0, 4.0)
    queries_out = jnp.clip(jax.random.normal(second_key, full_shape, jnp.float32), -4.0, 4.0)
    return (queries_out, keys_out)


def draw_queries(key, part):
    queries_out, keys_out = paired_draw(key)
    return queries_out.astype(jnp.bfloat16)


def draw_key_rows(key, part):
    queries_out, keys_out = paired_draw(key)
    return keys_out.astype(jnp.bfloat16)


def draw_pattern(key, part):
    owner_total = NBLK // QB_DEV
    block_ids = jnp.arange(NBLK, dtype=jnp.int32)
    before = (block_ids - 1 + NBLK) % NBLK
    after = (block_ids + 1) % NBLK
    key_first, key_second, key_perm, key_within = jax.random.split(jax.random.fold_in(key, 5), 4)
    first_global = jax.random.randint(key_first, (), 0, NBLK, dtype=jnp.int32)
    second_global = (first_global + jax.random.randint(key_second, (), 1, NBLK, dtype=jnp.int32)) % NBLK
    owner_keys = jax.random.split(key_perm, owner_total)
    orders = jax.vmap(lambda one_key: jax.random.permutation(one_key, owner_total))(owner_keys).astype(jnp.int32)
    request_pos = jnp.arange(QB_DEV * NRAND, dtype=jnp.int32) % owner_total
    owners = orders[:, request_pos]
    within = jax.random.randint(key_within, (owner_total, QB_DEV * NRAND), 0, QB_DEV, dtype=jnp.int32)
    picks = (owners * QB_DEV + within).reshape(NBLK, NRAND)
    globals_col = jnp.stack([jnp.full((NBLK,), first_global, jnp.int32), jnp.full((NBLK,), second_global, jnp.int32)], axis=1)
    return jnp.concatenate([jnp.stack([before, block_ids, after], axis=1), globals_col, picks], axis=1).astype(jnp.int32)


def levels(stream_key, shape, cuts, least, top_value):
    factor_of, own = 1.0, jax.random.fold_in(stream_key, 6)
    for dim, parts in cuts:
        steps = jnp.exp(jax.random.uniform(jax.random.fold_in(own, dim), (parts,), jnp.float32, least / len(cuts), top_value / len(cuts)))
        factor_of = factor_of * jnp.repeat(steps, shape[dim] // parts).reshape([-1 if axis == dim else 1 for axis in range(len(shape))])
    return factor_of


def centred(key, extent, deviation, limit, pieces=(), kind=jnp.bfloat16):
    factor_of = levels(key, extent, pieces, -0.22, 0.18) if pieces else 1.0
    values = jax.random.normal(key, extent, jnp.float32) * deviation * factor_of
    return jnp.minimum(jnp.maximum(values, -limit), limit).astype(kind)


def setup_inputs(seed: int = 0) -> dict:
    keys = jax.random.split(jax.random.key(seed), 7)
    return {
        "queries": draw_queries(jax.random.fold_in(keys[6], 71), 0),
        "key_rows": draw_key_rows(jax.random.fold_in(keys[6], 71), 0),
        "value_rows": centred(keys[2], (TOKENS, HEADS * HD), 1.0, 6.0, ((0, 32), (1, 8))),
        "pattern": draw_pattern(jax.random.fold_in(keys[6], 71), 0),
        "out_weight": centred(keys[4], (HD, HEADS, D), (HEADS * HD) ** -0.5, 0.109375, ((0, 32), (2, 8))),
        "out_grad": centred(keys[5], (TOKENS, D), 1.0, 6.0, ((0, 32), (1, 8))),
    }


HIGH = lax.Precision.HIGHEST

def as_float(array):
    return array.astype(jnp.float32)

def block_probs(query_block, key_set, score_scale):
    scores = jnp.einsum('qhd,khd->hqk', as_float(query_block), as_float(key_set), precision=HIGH) * score_scale
    probs = jax.nn.softmax(scores, axis=-1)
    return (probs, probs.astype(jnp.bfloat16))

def reference(queries, key_rows, value_rows, pattern, out_weight, out_grad):
    tok_total, width_all = queries.shape
    heads_all = width_all // HD
    block_total = tok_total // BLK
    score_scale = 1.0 / math.sqrt(HD)
    query_blocks = queries.reshape(block_total, BLK, heads_all, HD)
    key_blocks = key_rows.reshape(block_total, BLK, heads_all, HD)
    value_blocks = value_rows.reshape(block_total, BLK, heads_all, HD)

    def gather_set(blocks_in, picks):
        return jnp.take(blocks_in, picks, axis=0).reshape(NSEL * BLK, heads_all, HD)

    def attend(inputs):
        query_block, picks = inputs
        key_set = gather_set(key_blocks, picks)
        value_set = gather_set(value_blocks, picks)
        probs, probs_low = block_probs(query_block, key_set, score_scale)
        output = jnp.einsum('hqk,khd->qhd', as_float(probs_low), as_float(value_set), precision=HIGH)
        return output.astype(jnp.bfloat16)
    attended = lax.map(attend, (query_blocks, pattern)).reshape(tok_total, heads_all, HD)
    projected = jnp.einsum('the,ehc->tc', as_float(attended), as_float(out_weight), precision=HIGH).astype(jnp.bfloat16)
    group_cols = out_weight.shape[2] // N_FSDP
    head_grad = jnp.zeros((tok_total, heads_all, HD), jnp.float32)
    for group_index in range(N_FSDP):
        col_start = group_index * group_cols
        grad_cols = out_grad[:, col_start:col_start + group_cols]
        weight_cols = out_weight[:, :, col_start:col_start + group_cols]
        part_sum = jnp.einsum('tc,ehc->the', as_float(grad_cols), as_float(weight_cols), precision=HIGH)
        head_grad = head_grad + lax.optimization_barrier(part_sum.astype(jnp.bfloat16)).astype(jnp.float32)
    head_grad = head_grad.astype(jnp.bfloat16)
    owner_rows = tok_total // N_SEQ
    attended_owner = attended.reshape(N_SEQ, owner_rows, heads_all, HD)
    grad_owner = out_grad.reshape(N_SEQ, owner_rows, out_grad.shape[1])

    def add_owner(total, inputs):
        attn_part, grad_part = inputs
        term = jnp.einsum('the,tc->ehc', as_float(attn_part), as_float(grad_part), precision=HIGH)
        return (total + lax.optimization_barrier(term.astype(jnp.bfloat16)).astype(jnp.float32), None)
    weight_grad, unused = lax.scan(add_owner, jnp.zeros(out_weight.shape, jnp.float32), (attended_owner, grad_owner))
    grad_blocks = head_grad.reshape(block_total, BLK, heads_all, HD)

    def backward_block(carry, inputs):
        key_acc, value_acc = carry
        query_block, grad_block, picks = inputs
        key_set = gather_set(key_blocks, picks)
        value_set = gather_set(value_blocks, picks)
        probs, probs_low = block_probs(query_block, key_set, score_scale)
        prob_grad = jnp.einsum('qhd,khd->hqk', as_float(grad_block), as_float(value_set), precision=HIGH)
        center = lax.optimization_barrier(jnp.sum(probs * prob_grad, axis=-1, keepdims=True))
        score_grad = (probs * (prob_grad - center)).astype(jnp.bfloat16)
        query_out = (jnp.einsum('hqk,khd->qhd', as_float(score_grad), as_float(key_set), precision=HIGH) * score_scale).astype(jnp.bfloat16)
        key_terms = (jnp.einsum('hqk,qhd->khd', as_float(score_grad), as_float(query_block), precision=HIGH) * score_scale).astype(jnp.bfloat16)
        value_terms = jnp.einsum('hqk,qhd->khd', as_float(probs_low), as_float(grad_block), precision=HIGH).astype(jnp.bfloat16)
        key_acc = key_acc.at[picks].add(as_float(key_terms).reshape(NSEL, BLK, heads_all * HD))
        value_acc = value_acc.at[picks].add(as_float(value_terms).reshape(NSEL, BLK, heads_all * HD))
        return ((key_acc, value_acc), query_out)
    zero_acc = jnp.zeros((block_total, BLK, heads_all * HD), jnp.float32)
    (key_acc, value_acc), query_grad = lax.scan(backward_block, (zero_acc, zero_acc), (query_blocks, grad_blocks, pattern))
    query_grad = query_grad.reshape(tok_total, width_all)
    key_grad = key_acc.astype(jnp.bfloat16).reshape(tok_total, width_all)
    value_grad = value_acc.astype(jnp.bfloat16).reshape(tok_total, width_all)
    return (projected, query_grad, key_grad, value_grad, weight_grad)
```

```python
import functools
import math

import jax
import jax.numpy as jnp
from jax import lax
from jax.experimental import pallas as pl
from jax.experimental.pallas import tpu as pltpu
from jax.sharding import Mesh, PartitionSpec as P

HD = 128
BLK = 128
ROWS = 8
SEQ = ("y", "x", "core")
BF = jnp.bfloat16
F32 = jnp.float32
VMEM = pl.BlockSpec(memory_space=pltpu.VMEM)
SMEM = pl.BlockSpec(memory_space=pltpu.SMEM)
NT = (((1,), (1,)), ((), ()))
TN = (((0,), (0,)), ((), ()))


def dot(a, b, dims=(((1,), (0,)), ((), ()))):
    return lax.dot_general(a, b, dims, preferred_element_type=F32)


def call(kernel, out_shape, ins, flops, scratch=(), name=None):
    outs = out_shape if isinstance(out_shape, (tuple, list)) else [out_shape]
    moved = sum(math.prod(o.shape) * o.dtype.itemsize for o in outs) + sum(
        math.prod(i.shape) * i.dtype.itemsize for i in ins
    )
    multi = isinstance(out_shape, (tuple, list))
    return pl.pallas_call(
        kernel,
        out_shape=out_shape,
        in_specs=[SMEM if i.dtype == jnp.int32 else VMEM for i in ins],
        out_specs=[VMEM] * len(outs) if multi else VMEM,
        scratch_shapes=list(scratch),
        compiler_params=pltpu.CompilerParams(vmem_limit_bytes=48 << 20),
        cost_estimate=pl.CostEstimate(flops=flops, bytes_accessed=moved, transcendentals=0),
        name=name,
    )(*ins)


def shape(dims, dtype=BF):
    return jax.ShapeDtypeStruct(dims, dtype)


def shift(value, axis, by):
    n = lax.axis_size(axis)
    return lax.ppermute(value, axis, [(i, (i + by) % n) for i in range(n)])


def select_kernel(where, pieces, out):
    def body(i, carry):
        out[i] = pieces[where[i]]
        return carry

    lax.fori_loop(0, out.shape[0], body, 0, unroll=8)


def load_sets(own, prev, following, routed, which, j, dest):
    base = which * 16
    if j == 0:
        dest[0:BLK] = prev[which]
    else:
        dest[0:BLK] = own[0:BLK]
    dest[BLK : 2 * BLK] = own[j * BLK : (j + 1) * BLK]
    if j == 0:
        dest[2 * BLK : 3 * BLK] = own[BLK : 2 * BLK]
    else:
        dest[2 * BLK : 3 * BLK] = following[which]
    for slot in range(3, 8):
        place = slot - 3 if slot < 5 else slot - 3 + 3 * j
        dest[slot * BLK : (slot + 1) * BLK] = routed[base : base + 16, place].reshape(
            BLK, dest.shape[1]
        )


def forward_kernel(q, k, v, prev, following, routed, att, probs, kset, vset):
    scale = 1.0 / math.sqrt(HD)
    heads = q.shape[1] // HD
    for j in range(2):
        load_sets(k, prev, following, routed, 0, j, kset)
        load_sets(v, prev, following, routed, 1, j, vset)
        rows = pl.ds(j * BLK, BLK)
        for h in range(heads):
            cols = pl.ds(h * HD, HD)
            s = dot(q[rows, cols], kset[:, cols], NT) * scale
            e = jnp.exp(s - jnp.max(s, axis=-1, keepdims=True))
            p = e / jnp.sum(e, axis=-1, keepdims=True)
            probs[j * heads + h] = p
            att[rows, cols] = dot(p.astype(BF), vset[:, cols]).astype(BF)


def backward_kernel(
    q, k, v, prev, following, routed, probs, grad, qg, terms, edges, own, kset, vset, acc
):
    scale = 1.0 / math.sqrt(HD)
    heads = q.shape[1] // HD
    width = q.shape[1]
    for j in range(2):
        load_sets(k, prev, following, routed, 0, j, kset)
        load_sets(v, prev, following, routed, 1, j, vset)
        rows = pl.ds(j * BLK, BLK)
        for h in range(heads):
            cols = pl.ds(h * HD, HD)
            p = probs[j * heads + h]
            g = grad[rows, cols]
            pg = dot(g, vset[:, cols], NT)
            center = jnp.sum(p * pg, axis=-1, keepdims=True)
            sg = (p * (pg - center)).astype(BF)
            qg[rows, cols] = (dot(sg, kset[:, cols]) * scale).astype(BF)
            acc[0, :, cols] = dot(sg, q[rows, cols], TN) * scale
            acc[1, :, cols] = dot(p.astype(BF), g, TN)
        for which in range(2):
            t = lambda slot: acc[which, slot * BLK : (slot + 1) * BLK, :]
            cut = lambda a: a.astype(BF).reshape(16, ROWS, width)
            side = pl.ds(which * 16, 16)
            if j == 0:
                edges[0, which] = t(0).astype(BF)
                own[0, which] = t(1)
                own[1, which] = t(2)
            else:
                own[0, which] += t(0)
                own[1, which] += t(1)
                edges[1, which] = t(2).astype(BF)
            for slot in (3, 4):
                if j == 0:
                    terms[side, slot - 3] = cut(t(slot))
                else:
                    both = terms[side, slot - 3].reshape(BLK, width).astype(F32) + t(slot)
                    terms[side, slot - 3] = cut(both)
            for slot in (5, 6, 7):
                terms[side, slot - 3 + 3 * j] = cut(t(slot))


def gather_kernel(where, pieces, out, acc):
    acc[...] = jnp.zeros_like(acc)
    count = pieces.shape[0] // 8
    for slot in range(2):
        total = pieces[slot].astype(F32)
        for i in range(1, count):
            total = total + pieces[i * 8 + slot].astype(F32)
        acc[where[slot]] = total

    def body(i, carry):
        for slot in range(2, 8):
            at = where[i * 8 + slot]
            acc[at] = acc[at] + pieces[i * 8 + slot].astype(F32)
        return carry

    lax.fori_loop(0, count, body, 0, unroll=2)
    out[...] = acc[...].astype(BF)


def final_kernel(own, pieces, before, after, kg, vg):
    width = kg.shape[1]
    for which, out in ((0, kg), (1, vg)):
        for b in range(2):
            near = before[which] if b == 0 else after[which]
            far = pieces[which * 16 : which * 16 + 16, b].reshape(BLK, width)
            out[b * BLK : (b + 1) * BLK] = (
                own[b, which] + near.astype(F32) + far.astype(F32)
            ).astype(BF)


def head_part_kernel(place, g, *refs):
    parts, (weight, part) = refs[:-2], refs[-2:]
    me, yy, xx, cc = place[0], place[1], place[2], place[3]
    for first in range(2):
        for other in range(2):
            half = parts[(other * 2 + first) * 4 : (other * 2 + first) * 4 + 4]
            start = jnp.where(other == 0, cc, 1 - cc) * 12 + first * 6
            for far in range(4):
                ref = half[far]
                for near in range(4):
                    if first == 0:
                        yat, xat = lax.rem(yy + far, 4), lax.rem(xx + near, 4)
                    else:
                        yat, xat = lax.rem(yy + near, 4), lax.rem(xx + far, 4)
                    chip = yat * 4 + xat
                    for h in range(6):
                        weight[start + h, chip] = ref[near, h]
    for f in range(8):
        to = lax.rem(me + f, 8)
        w = weight[pl.ds(to * 3, 3)].reshape(3 * HD, weight.shape[3])
        part[f] = dot(g[...], w, NT).astype(BF)


def weight_grad_kernel(place, g, *refs):
    parts, out = refs[:-1], refs[-1]
    me = place[0]
    for f in range(8):
        at = lax.rem(me + f, 8)
        w = dot(parts[f][...], g[...], TN).astype(BF)
        out[pl.ds(at * 3, 3)] = w.reshape(3, 16, ROWS, w.shape[1])


def project_kernel(place, weight, *refs):
    parts, (out, acc) = refs[:-2], refs[-2:]
    me = place[0]
    for f in range(8):
        at = lax.rem(me + f, 8)
        w = weight[pl.ds(at * 3, 3)].reshape(3 * HD, weight.shape[3])
        term = dot(parts[f][...], w)
        acc[...] = term if f == 0 else acc[...] + term
    out[...] = acc[...].astype(BF)


def gather_four(v, axis):
    return [v, shift(v, axis, -1), shift(v, axis, 2), shift(v, axis, 1)]


def sum_four(v, axis, dim):
    me = lax.axis_index(axis)
    pick = lambda k: lax.dynamic_index_in_dim(v, (me + k) % 4, dim, keepdims=False)
    total = pick(0).astype(F32)
    for k in (2, 1, 3):
        total = total + shift(pick(k), axis, k).astype(F32)
    return total


def shards(queries, key_rows, value_rows, pattern, out_weight, out_grad):
    width = queries.shape[1]
    core = lax.axis_index("core")
    z = lax.axis_index("z")
    place = jnp.stack([z, lax.axis_index("y"), lax.axis_index("x"), core]).astype(jnp.int32)
    feats = out_weight.shape[2]

    kv = jnp.stack([key_rows.reshape(2, BLK, width), value_rows.reshape(2, BLK, width)], axis=1)
    pieces = kv.reshape(2, 32, ROWS, width).transpose(1, 0, 2, 3)
    wanted = pattern[:, 5:].reshape(1, 1, 1, 6).astype(BF)
    wanted = jnp.pad(wanted, ((0, 0), (0, 0), (0, ROWS - 1), (0, width - 6)))
    sent = jnp.concatenate([pieces, jnp.broadcast_to(wanted, (32, 1, ROWS, width))], axis=1)
    spread = lax.all_to_all(sent, SEQ, split_axis=0, concat_axis=0, tiled=True)
    prev = shift(kv[1], SEQ, 1)
    following = shift(kv[0], SEQ, -1)

    mine = lax.dynamic_slice_in_dim(out_weight, core * 12, 12, axis=1)
    theirs = shift(lax.dynamic_slice_in_dim(out_weight, 12 - core * 12, 12, axis=1), "core", 1)
    chip = jnp.where(
        core == 0, jnp.concatenate([mine, theirs], 0), jnp.concatenate([theirs, mine], 0)
    ).transpose(1, 0, 2)
    near_a = jnp.stack(gather_four(chip[:6], "x"), 0)
    near_b = jnp.stack(gather_four(chip[6:], "y"), 0)
    own_parts = gather_four(near_a, "y") + gather_four(near_b, "x")
    parts = own_parts + [shift(p, "core", 1) for p in own_parts]
    weight, part = call(
        head_part_kernel,
        [shape((24, 16, ROWS, feats)), shape((8, 2 * BLK, width))],
        [place, out_grad, *parts],
        2 * 256 * 3072 * 768,
        name="head_part",
    )

    ids = spread[:, 2, 0, :6].astype(jnp.int32)
    global_ids = jnp.broadcast_to(pattern[0:1, 3:5], (32, 2))
    block_of = jnp.concatenate([global_ids, ids], axis=1).reshape(256)
    routed = call(
        select_kernel,
        shape((256, ROWS, width)),
        [(block_of // 2) * 3 + block_of % 2, spread.reshape(96, ROWS, width)],
        1000,
        name="select",
    )
    routed = lax.all_to_all(
        routed.reshape(32, 8, ROWS, width), SEQ, split_axis=0, concat_axis=0, tiled=True
    )
    sets = [pltpu.VMEM((8 * BLK, width), BF)] * 2
    attended, probs = call(
        forward_kernel,
        [shape((2 * BLK, width)), shape((6, BLK, 8 * BLK), F32)],
        [queries, key_rows, value_rows, prev, following, routed],
        2 * 2 * 6 * 128 * 1024 * 128,
        sets,
        name="attention_forward",
    )

    half = BLK
    right = shift(part[4][:half], "z", 1)
    left = shift(part[4][half:], "z", -1)
    add = lambda a, b: (a.astype(F32) + b.astype(F32)).astype(BF)
    right = jnp.concatenate([add(part[3][:half], right), part[3][half:]], 0)
    left = jnp.concatenate([part[5][:half], add(part[5][half:], left)], 0)
    right, left = shift(right, "z", 1), shift(left, "z", -1)
    right, left = add(part[2], right), add(part[6], left)
    right, left = shift(right, "z", 1), shift(left, "z", -1)
    right, left = add(part[1], right), add(part[7], left)
    right, left = shift(right, "z", 1), shift(left, "z", -1)
    head_grad = (part[0].astype(F32) + right.astype(F32) + left.astype(F32)).astype(BF)

    rel = {0: attended}
    ahead = behind = attended
    for k in (1, 2, 3):
        ahead, behind = shift(ahead, "z", -1), shift(behind, "z", 1)
        rel[k], rel[8 - k] = ahead, behind
    rel[4] = jnp.concatenate([shift(ahead[:half], "z", -1), shift(behind[half:], "z", 1)], 0)
    rel = [rel[k] for k in range(8)]

    local = call(
        weight_grad_kernel,
        shape((24, 16, ROWS, feats)),
        [place, out_grad, *rel],
        2 * 256 * 3072 * 768,
        name="weight_grad",
    )
    projected = call(
        project_kernel,
        shape((2 * BLK, feats)),
        [place, weight, *rel],
        2 * 256 * 3072 * 768,
        [pltpu.VMEM((2 * BLK, feats), F32)],
        name="project",
    )

    query_grad, terms, edges, own = call(
        backward_kernel,
        [
            shape((2 * BLK, width)),
            shape((32, 8, ROWS, width)),
            shape((2, 2, BLK, width)),
            shape((2, 2, BLK, width), F32),
        ],
        [queries, key_rows, value_rows, prev, following, routed, probs, head_grad],
        5 * 2 * 6 * 128 * 1024 * 128,
        sets + [pltpu.VMEM((2, 8 * BLK, width), F32)],
        name="attention_backward",
    )
    terms = lax.all_to_all(terms, SEQ, split_axis=0, concat_axis=0, tiled=True)
    after = shift(edges[0], SEQ, -1)
    before = shift(edges[1], SEQ, 1)
    sums = call(
        gather_kernel,
        shape((64, ROWS, width)),
        [block_of, terms.reshape(256, ROWS, width)],
        1000,
        [pltpu.VMEM((64, ROWS, width), F32)],
        name="gather",
    )
    back = lax.all_to_all(
        sums.reshape(32, 2, ROWS, width), SEQ, split_axis=0, concat_axis=0, tiled=True
    )
    key_grad, value_grad = call(
        final_kernel,
        [shape((2 * BLK, width)), shape((2 * BLK, width))],
        [own, back, before, after],
        1000,
        name="final",
    )

    kept = lax.dynamic_slice_in_dim(local, core * 12, 12, axis=0)
    given = shift(lax.dynamic_slice_in_dim(local, 12 - core * 12, 12, axis=0), "core", 1)
    pair = add(kept, given).reshape(12, 4, 4, ROWS, feats)
    sum_a = sum_four(sum_four(pair[:6], "x", 2).astype(BF), "y", 1)
    sum_b = sum_four(sum_four(pair[6:], "y", 1).astype(BF), "x", 1)
    total = jnp.concatenate([sum_a, sum_b], 0)
    stay = lax.dynamic_slice_in_dim(total, core * 4, 4, axis=1)
    leave = lax.dynamic_slice_in_dim(total, 4 - core * 4, 4, axis=1)
    came = shift(leave.astype(BF), "core", 1).astype(F32)
    weight_grad = jnp.where(
        core == 0, jnp.concatenate([stay, came], 0), jnp.concatenate([came, stay], 0)
    ).transpose(1, 0, 2)
    return (projected, query_grad, key_grad, value_grad, weight_grad)


def solution(mesh):
    split = Mesh(mesh.devices.reshape(4, 4, 2, 8), ("y", "x", "core", "z"))
    rows, cols = ("y", "x", "core"), "z"
    return jax.shard_map(
        shards,
        mesh=split,
        in_specs=(
            P(rows, cols),
            P(rows, cols),
            P(rows, cols),
            P(rows, None),
            P(rows, None, cols),
            P(rows, cols),
        ),
        out_specs=(
            P(rows, cols),
            P(rows, cols),
            P(rows, cols),
            P(rows, cols),
            P(rows, None, cols),
        ),
        check_vma=False,
    )
```

```python
import math

import jax
import jax.numpy as jnp
from jax import lax
from jax.experimental import pallas as pl
from jax.experimental.pallas import tpu as pltpu
from jax.sharding import Mesh, PartitionSpec as P

HD = 128
BLK = 128
ROWS = 8
SEQ = ("y", "x", "core")
BF = jnp.bfloat16
F32 = jnp.float32
VMEM = pl.BlockSpec(memory_space=pltpu.VMEM)
HBM = pl.BlockSpec(memory_space=pl.ANY)
SMEM = pl.BlockSpec(memory_space=pltpu.SMEM)
NT = (((1,), (1,)), ((), ()))
TN = (((0,), (0,)), ((), ()))


def dot(a, b, dims=(((1,), (0,)), ((), ()))):
    return lax.dot_general(a, b, dims, preferred_element_type=F32)


def call(kernel, out_shape, ins, flops, scratch=(), name=None, far=(), vmem=16, out=VMEM):
    outs = out_shape if isinstance(out_shape, (tuple, list)) else [out_shape]
    moved = sum(math.prod(o.shape) * o.dtype.itemsize for o in outs) + sum(
        math.prod(i.shape) * i.dtype.itemsize for i in ins
    )
    multi = isinstance(out_shape, (tuple, list))
    return pl.pallas_call(
        kernel,
        out_shape=out_shape,
        in_specs=[SMEM if i.dtype == jnp.int32 else VMEM for i in ins]
        + [HBM] * len(far),
        out_specs=[out] * len(outs) if multi else out,
        scratch_shapes=list(scratch),
        compiler_params=pltpu.CompilerParams(vmem_limit_bytes=vmem << 20),
        cost_estimate=pl.CostEstimate(flops=flops, bytes_accessed=moved, transcendentals=0),
        name=name,
    )(*ins, *far)


def shape(dims, dtype=BF):
    return jax.ShapeDtypeStruct(dims, dtype)


def shift(value, axis, by):
    n = lax.axis_size(axis)
    return lax.ppermute(value, axis, [(i, (i + by) % n) for i in range(n)])


def select_kernel(where, pieces, *refs):
    out = refs[-1]

    def body(i, carry):
        out[i] = pieces[where[i]]
        return carry

    lax.fori_loop(0, out.shape[0], body, 0, unroll=8)


def load_sets(own, prev, following, routed, which, j, dest):
    base = which * 16
    if j == 0:
        dest[0:BLK] = prev[which]
    else:
        dest[0:BLK] = own[0:BLK]
    dest[BLK : 2 * BLK] = own[j * BLK : (j + 1) * BLK]
    if j == 0:
        dest[2 * BLK : 3 * BLK] = own[BLK : 2 * BLK]
    else:
        dest[2 * BLK : 3 * BLK] = following[which]
    for slot in range(3, 8):
        place = slot - 3 if slot < 5 else slot - 3 + 3 * j
        dest[slot * BLK : (slot + 1) * BLK] = routed[base : base + 16, place].reshape(
            BLK, dest.shape[1]
        )


def forward_kernel(q, k, v, prev, following, routed, _p, att, probs, kset, vset):
    scale = 1.0 / math.sqrt(HD)
    heads = q.shape[1] // HD
    for j in range(2):
        load_sets(k, prev, following, routed, 0, j, kset)
        load_sets(v, prev, following, routed, 1, j, vset)
        rows = pl.ds(j * BLK, BLK)
        for h in range(heads):
            cols = pl.ds(h * HD, HD)
            s = dot(q[rows, cols], kset[:, cols], NT) * scale
            e = jnp.exp(s - jnp.max(s, axis=-1, keepdims=True))
            p = e / jnp.sum(e, axis=-1, keepdims=True)
            probs[j * heads + h] = p
            att[rows, cols] = dot(p.astype(BF), vset[:, cols]).astype(BF)


def backward_kernel(
    q, k, v, prev, following, routed, probs, grad, qg, terms, edges, own, kset, vset, acc
):
    scale = 1.0 / math.sqrt(HD)
    heads = q.shape[1] // HD
    width = q.shape[1]
    for j in range(2):
        load_sets(k, prev, following, routed, 0, j, kset)
        load_sets(v, prev, following, routed, 1, j, vset)
        rows = pl.ds(j * BLK, BLK)
        for h in range(heads):
            cols = pl.ds(h * HD, HD)
            p = probs[j * heads + h]
            g = grad[rows, cols]
            pg = dot(g, vset[:, cols], NT)
            center = jnp.sum(p * pg, axis=-1, keepdims=True)
            sg = (p * (pg - center)).astype(BF)
            qg[rows, cols] = (dot(sg, kset[:, cols]) * scale).astype(BF)
            acc[0, :, cols] = dot(sg, q[rows, cols], TN) * scale
            acc[1, :, cols] = dot(p.astype(BF), g, TN)
        for which in range(2):
            t = lambda slot: acc[which, slot * BLK : (slot + 1) * BLK, :]
            cut = lambda a: a.astype(BF).reshape(16, ROWS, width)
            side = pl.ds(which * 16, 16)
            if j == 0:
                edges[0, which] = t(0).astype(BF)
                own[0, which] = t(1)
                own[1, which] = t(2)
            else:
                own[0, which] += t(0)
                own[1, which] += t(1)
                edges[1, which] = t(2).astype(BF)
            for slot in (3, 4):
                if j == 0:
                    terms[side, slot - 3] = cut(t(slot))
                else:
                    both = terms[side, slot - 3].reshape(BLK, width).astype(F32) + t(slot)
                    terms[side, slot - 3] = cut(both)
            for slot in (5, 6, 7):
                terms[side, slot - 3 + 3 * j] = cut(t(slot))


def gather_kernel(where, pieces, out, acc):
    acc[...] = jnp.zeros_like(acc)
    count = pieces.shape[0] // 8
    for slot in range(2):
        total = pieces[slot].astype(F32)
        for i in range(1, count):
            total = total + pieces[i * 8 + slot].astype(F32)
        acc[where[slot]] = total

    def body(i, carry):
        for slot in range(2, 8):
            at = where[i * 8 + slot]
            acc[at] = acc[at] + pieces[i * 8 + slot].astype(F32)
        return carry

    lax.fori_loop(0, count, body, 0, unroll=2)
    out[...] = acc[...].astype(BF)


def final_kernel(own, pieces, before, after, kg, vg):
    width = kg.shape[1]
    for which, out in ((0, kg), (1, vg)):
        for b in range(2):
            near = before[which] if b == 0 else after[which]
            far = pieces[which * 16 : which * 16 + 16, b].reshape(BLK, width)
            out[b * BLK : (b + 1) * BLK] = (
                own[b, which] + near.astype(F32) + far.astype(F32)
            ).astype(BF)


def load_weight(place, parts, weight, sems):
    yy, xx, cc = place[1], place[2], place[3]
    copies = []
    for first in range(2):
        for other in range(2):
            half = parts[(other * 2 + first) * 4 : (other * 2 + first) * 4 + 4]
            start = (cc if other == 0 else 1 - cc) * 12 + first * 6
            for far in range(4):
                for near in range(4):
                    if first == 0:
                        yat, xat = lax.rem(yy + far, 4), lax.rem(xx + near, 4)
                    else:
                        yat, xat = lax.rem(yy + near, 4), lax.rem(xx + far, 4)
                    copies.append(
                        pltpu.make_async_copy(
                            half[far].at[near],
                            weight.at[pl.ds(start, 6), yat * 4 + xat],
                            sems.at[len(copies)],
                        )
                    )
    for copy in copies:
        copy.start()
    return copies


def head_part_kernel(place, *refs):
    g_far, parts, part, (g, weight, sums, sems, out_sems) = refs[0], refs[1:17], refs[17:25], refs[25:]
    take = pltpu.make_async_copy(g_far, g, sems.at[64])
    take.start()
    copies = load_weight(place, parts, weight, sems)
    take.wait()
    for copy in copies:
        copy.wait()
    leaving = []
    for f in (4, 3, 5, 2, 6, 1, 7, 0):
        to = lax.rem(place[0] + f, 8)
        w = weight[pl.ds(to * 3, 3)].reshape(3 * HD, weight.shape[3])
        sums[f] = dot(g[...], w, NT).astype(BF)
        leaving.append(pltpu.make_async_copy(sums.at[f], part[f], out_sems.at[f]))
        leaving[-1].start()
    for copy in leaving:
        copy.wait()


def weight_grad_kernel(place, *refs):
    g_far, parts, (kept, given), (g, held, made, sems, out_sems) = (
        refs[0],
        refs[1:9],
        refs[10:12],
        refs[12:],
    )
    me, cc = place[0], place[3]
    copies = [pltpu.make_async_copy(g_far, g, sems.at[8])]
    copies += [pltpu.make_async_copy(parts[f], held.at[f], sems.at[f]) for f in range(8)]
    for copy in copies:
        copy.start()
    copies[0].wait()
    leaving = []
    for f in range(8):
        copies[f + 1].wait()
        at = lax.rem(me + f, 8)
        made[f] = dot(held[f], g[...], TN).astype(BF).reshape(3, 16, ROWS, g.shape[1])
        spot = pl.ds(lax.rem(at, 4) * 3, 3)
        keep = pltpu.make_async_copy(made.at[f], kept.at[spot], out_sems.at[f])
        give = pltpu.make_async_copy(made.at[f], given.at[spot], out_sems.at[f])

        @pl.when(at // 4 == cc)
        def start_keep():
            keep.start()

        @pl.when(at // 4 != cc)
        def start_give():
            give.start()

        leaving.append(keep)
    for copy in leaving:
        copy.wait()


def pair_kernel(place, *refs):
    yy, xx = place[1], place[2]
    kept_a, given_a, kept_b, given_b = refs[:4]
    out_a, out_b = refs[4:8], refs[8:12]
    for k in range(4):
        xat, yat = lax.rem(xx + k, 4), lax.rem(yy + k, 4)
        for i in range(4):
            at = i * 4 + xat
            out_a[k][:, i] = (kept_a[:, at].astype(F32) + given_a[:, at].astype(F32)).astype(BF)
            at = yat * 4 + i
            out_b[k][:, i] = (kept_b[:, at].astype(F32) + given_b[:, at].astype(F32)).astype(BF)


def middle_kernel(place, *refs):
    yy, xx = place[1], place[2]
    for ins, outs, at in ((refs[:4], refs[8:12], yy), (refs[4:8], refs[12:16], xx)):
        for k in range(4):
            to = lax.rem(at + k, 4)
            total = ins[0][:, to].astype(F32)
            for i in (1, 2, 3):
                total = total + ins[i][:, to].astype(F32)
            outs[k][...] = total.astype(BF)


def last_kernel(*refs):
    out = refs[8]
    for first in range(2):
        total = refs[first * 4][...].astype(F32)
        for i in (1, 2, 3):
            total = total + refs[first * 4 + i][...].astype(F32)
        out[first * 6 : first * 6 + 6] = total


def by_head(dims, at=0):
    return pl.BlockSpec((3, *dims), lambda h, *_: (h + at, *([0] * len(dims))))


def gridded(kernel, outs, specs, ins, place, name):
    moved = sum(math.prod(o.shape) * o.dtype.itemsize for o in outs) + sum(
        math.prod(i.shape) * i.dtype.itemsize for i in ins
    )
    return pl.pallas_call(
        kernel,
        grid_spec=pltpu.PrefetchScalarGridSpec(
            num_scalar_prefetch=1,
            grid=(2,),
            in_specs=specs,
            out_specs=[by_head(o.shape[1:]) for o in outs],
        ),
        out_shape=[pltpu.HBM(o.shape, o.dtype) for o in outs],
        compiler_params=pltpu.CompilerParams(vmem_limit_bytes=56 << 20),
        cost_estimate=pl.CostEstimate(flops=1000, bytes_accessed=moved, transcendentals=0),
        name=name,
    )(place, *ins)


def project_kernel(place, *refs):
    rel, parts, out, (held, weight, acc, sems) = refs[:8], refs[8:24], refs[24], refs[25:]
    copies = load_weight(place, parts, weight, sems)
    copies += [pltpu.make_async_copy(rel[f], held.at[f], sems.at[64 + f]) for f in range(8)]
    for copy in copies[64:]:
        copy.start()
    for copy in copies:
        copy.wait()
    for f in range(8):
        at = lax.rem(place[0] + f, 8)
        w = weight[pl.ds(at * 3, 3)].reshape(3 * HD, weight.shape[3])
        term = dot(held[f], w)
        acc[...] = term if f == 0 else acc[...] + term
    out[...] = acc[...].astype(BF)


def gather_four(v, axis):
    return [v, shift(v, axis, -1), shift(v, axis, 2), shift(v, axis, 1)]


def shards(queries, key_rows, value_rows, pattern, out_weight, out_grad):
    width = queries.shape[1]
    core = lax.axis_index("core")
    z = lax.axis_index("z")
    place = jnp.stack([z, lax.axis_index("y"), lax.axis_index("x"), core]).astype(jnp.int32)
    feats = out_weight.shape[2]

    kv = jnp.stack([key_rows.reshape(2, BLK, width), value_rows.reshape(2, BLK, width)], axis=1)
    pieces = kv.reshape(2, 32, ROWS, width).transpose(1, 0, 2, 3)
    wanted = pattern[:, 5:].reshape(1, 1, 1, 6).astype(BF)
    wanted = jnp.pad(wanted, ((0, 0), (0, 0), (0, ROWS - 1), (0, width - 6)))
    sent = jnp.concatenate([pieces, jnp.broadcast_to(wanted, (32, 1, ROWS, width))], axis=1)
    prev = shift(kv[1], SEQ, 1)
    following = shift(kv[0], SEQ, -1)
    spread = lax.all_to_all(sent, SEQ, split_axis=0, concat_axis=0, tiled=True)

    mine = lax.dynamic_slice_in_dim(out_weight, core * 12, 12, axis=1)
    theirs = shift(lax.dynamic_slice_in_dim(out_weight, 12 - core * 12, 12, axis=1), "core", 1)
    chip = jnp.where(
        core == 0, jnp.concatenate([mine, theirs], 0), jnp.concatenate([theirs, mine], 0)
    ).transpose(1, 0, 2)
    near_a = jnp.stack(gather_four(chip[:6], "x"), 0)
    near_b = jnp.stack(gather_four(chip[6:], "y"), 0)
    own_parts = gather_four(near_a, "y") + gather_four(near_b, "x")
    parts = own_parts + [shift(p, "core", 1) for p in own_parts]
    part = call(
        head_part_kernel,
        [shape((2 * BLK, width))] * 8,
        [place],
        2 * 256 * 3072 * 768,
        [
            pltpu.VMEM((2 * BLK, feats), BF),
            pltpu.VMEM((24, 16, ROWS, feats), BF),
            pltpu.VMEM((8, 2 * BLK, width), BF),
            pltpu.SemaphoreType.DMA((65,)),
            pltpu.SemaphoreType.DMA((8,)),
        ],
        name="head_part",
        far=[out_grad, *parts],
        vmem=56,
        out=HBM,
    )

    ids = spread[:, 2, 0, :6].astype(jnp.int32)
    global_ids = jnp.broadcast_to(pattern[0:1, 3:5], (32, 2))
    block_of = jnp.concatenate([global_ids, ids], axis=1).reshape(256)
    routed = call(
        select_kernel,
        shape((256, ROWS, width)),
        [(block_of // 2) * 3 + block_of % 2, spread.reshape(96, ROWS, width)],
        1000,
        name="select",
        far=[near_a, near_b, prev, following],
    )
    routed = lax.all_to_all(
        routed.reshape(32, 8, ROWS, width), SEQ, split_axis=0, concat_axis=0, tiled=True
    )
    sets = [pltpu.VMEM((8 * BLK, width), BF)] * 2
    attended, probs = call(
        forward_kernel,
        [shape((2 * BLK, width)), shape((6, BLK, 8 * BLK), F32)],
        [queries, key_rows, value_rows, prev, following, routed],
        2 * 2 * 6 * 128 * 1024 * 128,
        sets,
        name="attention_forward",
        far=[part[0]],
    )

    half = BLK
    add = lambda a, b: (a.astype(F32) + b.astype(F32)).astype(BF)
    pass_on = lambda pair: (shift(pair[0], "z", 1), shift(pair[1], "z", -1))
    right, left = pass_on((part[4][:half], part[4][half:]))
    right = jnp.concatenate([add(part[3][:half], right), part[3][half:]], 0)
    left = jnp.concatenate([part[5][:half], add(part[5][half:], left)], 0)
    rel = {0: attended}
    ahead = behind = attended
    for k in (1, 2, 3):
        right, left = pass_on((right, left))
        if k < 3:
            right, left = add(part[3 - k], right), add(part[5 + k], left)
        ahead, behind = shift(ahead, "z", -1), shift(behind, "z", 1)
        rel[k], rel[8 - k] = ahead, behind
        right, left, ahead, behind = lax.optimization_barrier((right, left, ahead, behind))
    head_grad = (part[0].astype(F32) + right.astype(F32) + left.astype(F32)).astype(BF)
    rel[4] = jnp.concatenate([shift(ahead[:half], "z", -1), shift(behind[half:], "z", 1)], 0)
    rel = [rel[k] for k in range(8)]

    query_grad, terms, edges, own = call(
        backward_kernel,
        [
            shape((2 * BLK, width)),
            shape((32, 8, ROWS, width)),
            shape((2, 2, BLK, width)),
            shape((2, 2, BLK, width), F32),
        ],
        [queries, key_rows, value_rows, prev, following, routed, probs, head_grad],
        5 * 2 * 6 * 128 * 1024 * 128,
        sets + [pltpu.VMEM((2, 8 * BLK, width), F32)],
        name="attention_backward",
    )
    kept, given = call(
        weight_grad_kernel,
        [shape((12, 16, ROWS, feats))] * 2,
        [place],
        2 * 256 * 3072 * 768,
        [
            pltpu.VMEM((2 * BLK, feats), BF),
            pltpu.VMEM((8, 2 * BLK, width), BF),
            pltpu.VMEM((8, 3, 16, ROWS, feats), BF),
            pltpu.SemaphoreType.DMA((9,)),
            pltpu.SemaphoreType.DMA((8,)),
        ],
        name="weight_grad",
        far=[out_grad, *rel, edges],
        vmem=56,
        out=HBM,
    )
    projected = call(
        project_kernel,
        shape((2 * BLK, feats)),
        [place],
        2 * 256 * 3072 * 768,
        [
            pltpu.VMEM((8, 2 * BLK, width), BF),
            pltpu.VMEM((24, 16, ROWS, feats), BF),
            pltpu.VMEM((2 * BLK, feats), F32),
            pltpu.SemaphoreType.DMA((72,)),
        ],
        name="project",
        far=[*rel, *parts],
        vmem=56,
    )

    terms = lax.all_to_all(terms, SEQ, split_axis=0, concat_axis=0, tiled=True)
    after = shift(edges[0], SEQ, -1)
    before = shift(edges[1], SEQ, 1)
    sums = call(
        gather_kernel,
        shape((64, ROWS, width)),
        [block_of, terms.reshape(256, ROWS, width)],
        1000,
        [pltpu.VMEM((64, ROWS, width), F32)],
        name="gather",
    )
    back = lax.all_to_all(
        sums.reshape(32, 2, ROWS, width), SEQ, split_axis=0, concat_axis=0, tiled=True
    )
    key_grad, value_grad = call(
        final_kernel,
        [shape((2 * BLK, width)), shape((2 * BLK, width))],
        [own, back, before, after],
        1000,
        name="final",
    )

    given = shift(given, "core", 1)
    whole = (16, ROWS, feats)
    pair = gridded(
        pair_kernel,
        [shape((6, 4, ROWS, feats))] * 8,
        [by_head(whole), by_head(whole), by_head(whole, 2), by_head(whole, 2)],
        [kept, given, kept, given],
        place,
        "pair",
    )
    send = lambda v, axis: [v[0]] + [shift(v[k], axis, k) for k in (1, 2, 3)]
    middle = gridded(
        middle_kernel,
        [shape((6, ROWS, feats))] * 8,
        [by_head((4, ROWS, feats))] * 8,
        send(pair[:4], "x") + send(pair[4:], "y"),
        place,
        "middle",
    )
    total = call(
        last_kernel,
        shape((12, ROWS, feats), F32),
        send(middle[:4], "y") + send(middle[4:], "x"),
        1000,
        name="last",
    )
    stay = lax.dynamic_slice_in_dim(total, core * 4, 4, axis=1)
    leave = lax.dynamic_slice_in_dim(total, 4 - core * 4, 4, axis=1)
    came = shift(leave.astype(BF), "core", 1).astype(F32)
    weight_grad = jnp.where(
        core == 0, jnp.concatenate([stay, came], 0), jnp.concatenate([came, stay], 0)
    ).transpose(1, 0, 2)
    return (projected, query_grad, key_grad, value_grad, weight_grad)


def solution(mesh):
    split = Mesh(mesh.devices.reshape(4, 4, 2, 8), ("y", "x", "core", "z"))
    rows, cols = ("y", "x", "core"), "z"
    return jax.shard_map(
        shards,
        mesh=split,
        in_specs=(
            P(rows, cols),
            P(rows, cols),
            P(rows, cols),
            P(rows, None),
            P(rows, None, cols),
            P(rows, cols),
        ),
        out_specs=(
            P(rows, cols),
            P(rows, cols),
            P(rows, cols),
            P(rows, cols),
            P(rows, None, cols),
        ),
        check_vma=False,
    )
```

```python
import math

import jax
import jax.numpy as jnp
from jax import lax
from jax.experimental import pallas as pl
from jax.experimental.pallas import tpu as pltpu
from jax.sharding import Mesh, PartitionSpec as P

HD = 128
BLK = 128
ROWS = 8
SEQ = ("y", "x", "core")
BF = jnp.bfloat16
F32 = jnp.float32
VMEM = pl.BlockSpec(memory_space=pltpu.VMEM)
HBM = pl.BlockSpec(memory_space=pl.ANY)
SMEM = pl.BlockSpec(memory_space=pltpu.SMEM)
NT = (((1,), (1,)), ((), ()))
TN = (((0,), (0,)), ((), ()))


def dot(a, b, dims=(((1,), (0,)), ((), ()))):
    return lax.dot_general(a, b, dims, preferred_element_type=F32)


def call(kernel, out_shape, ins, flops, scratch=(), name=None, far=(), vmem=16, out=VMEM):
    outs = out_shape if isinstance(out_shape, (tuple, list)) else [out_shape]
    moved = sum(math.prod(o.shape) * o.dtype.itemsize for o in outs) + sum(
        math.prod(i.shape) * i.dtype.itemsize for i in ins
    )
    multi = isinstance(out_shape, (tuple, list))
    return pl.pallas_call(
        kernel,
        out_shape=out_shape,
        in_specs=[SMEM if i.dtype == jnp.int32 else VMEM for i in ins]
        + [HBM] * len(far),
        out_specs=[out] * len(outs) if multi else out,
        scratch_shapes=list(scratch),
        compiler_params=pltpu.CompilerParams(vmem_limit_bytes=vmem << 20),
        cost_estimate=pl.CostEstimate(flops=flops, bytes_accessed=moved, transcendentals=0),
        name=name,
    )(*ins, *far)


def shape(dims, dtype=BF):
    return jax.ShapeDtypeStruct(dims, dtype)


def shift(value, axis, by):
    n = lax.axis_size(axis)
    return lax.ppermute(value, axis, [(i, (i + by) % n) for i in range(n)])


def select_kernel(where, pieces, *refs):
    out = refs[-1]

    def body(i, carry):
        out[i] = pieces[where[i]]
        return carry

    lax.fori_loop(0, out.shape[0], body, 0, unroll=8)


def load_sets(own, prev, following, routed, which, j, dest):
    base = which * 16
    if j == 0:
        dest[0:BLK] = prev[which]
    else:
        dest[0:BLK] = own[0:BLK]
    dest[BLK : 2 * BLK] = own[j * BLK : (j + 1) * BLK]
    if j == 0:
        dest[2 * BLK : 3 * BLK] = own[BLK : 2 * BLK]
    else:
        dest[2 * BLK : 3 * BLK] = following[which]
    for slot in range(3, 8):
        place = slot - 3 if slot < 5 else slot - 3 + 3 * j
        dest[slot * BLK : (slot + 1) * BLK] = routed[base : base + 16, place].reshape(
            BLK, dest.shape[1]
        )


def forward_kernel(q, k, v, prev, following, routed, _p, att, probs, kset, vset):
    scale = 1.0 / math.sqrt(HD)
    heads = q.shape[1] // HD
    for j in range(2):
        load_sets(k, prev, following, routed, 0, j, kset)
        load_sets(v, prev, following, routed, 1, j, vset)
        rows = pl.ds(j * BLK, BLK)
        for h in range(heads):
            cols = pl.ds(h * HD, HD)
            s = dot(q[rows, cols], kset[:, cols], NT) * scale
            e = jnp.exp(s - jnp.max(s, axis=-1, keepdims=True))
            p = e / jnp.sum(e, axis=-1, keepdims=True)
            probs[j * heads + h] = p
            att[rows, cols] = dot(p.astype(BF), vset[:, cols]).astype(BF)


def backward_kernel(
    q, k, v, prev, following, routed, probs, grad, qg, terms, edges, own, kset, vset, acc
):
    scale = 1.0 / math.sqrt(HD)
    heads = q.shape[1] // HD
    width = q.shape[1]
    for j in range(2):
        load_sets(k, prev, following, routed, 0, j, kset)
        load_sets(v, prev, following, routed, 1, j, vset)
        rows = pl.ds(j * BLK, BLK)
        for h in range(heads):
            cols = pl.ds(h * HD, HD)
            p = probs[j * heads + h]
            g = grad[rows, cols]
            pg = dot(g, vset[:, cols], NT)
            center = jnp.sum(p * pg, axis=-1, keepdims=True)
            sg = (p * (pg - center)).astype(BF)
            qg[rows, cols] = (dot(sg, kset[:, cols]) * scale).astype(BF)
            acc[0, :, cols] = dot(sg, q[rows, cols], TN) * scale
            acc[1, :, cols] = dot(p.astype(BF), g, TN)
        for which in range(2):
            t = lambda slot: acc[which, slot * BLK : (slot + 1) * BLK, :]
            cut = lambda a: a.astype(BF).reshape(16, ROWS, width)
            side = pl.ds(which * 16, 16)
            if j == 0:
                edges[0, which] = t(0).astype(BF)
                own[0, which] = t(1)
                own[1, which] = t(2)
            else:
                own[0, which] += t(0)
                own[1, which] += t(1)
                edges[1, which] = t(2).astype(BF)
            for slot in (3, 4):
                if j == 0:
                    terms[side, slot - 3] = cut(t(slot))
                else:
                    both = terms[side, slot - 3].reshape(BLK, width).astype(F32) + t(slot)
                    terms[side, slot - 3] = cut(both)
            for slot in (5, 6, 7):
                terms[side, slot - 3 + 3 * j] = cut(t(slot))


def gather_kernel(where, pieces, out, acc):
    acc[...] = jnp.zeros_like(acc)
    count = pieces.shape[0] // 8
    for slot in range(2):
        total = pieces[slot].astype(F32)
        for i in range(1, count):
            total = total + pieces[i * 8 + slot].astype(F32)
        acc[where[slot]] = total

    def body(i, carry):
        for slot in range(2, 8):
            at = where[i * 8 + slot]
            acc[at] = acc[at] + pieces[i * 8 + slot].astype(F32)
        return carry

    lax.fori_loop(0, count, body, 0, unroll=2)
    out[...] = acc[...].astype(BF)


def final_kernel(own, pieces, before, after, kg, vg):
    width = kg.shape[1]
    for which, out in ((0, kg), (1, vg)):
        for b in range(2):
            near = before[which] if b == 0 else after[which]
            far = pieces[which * 16 : which * 16 + 16, b].reshape(BLK, width)
            out[b * BLK : (b + 1) * BLK] = (
                own[b, which] + near.astype(F32) + far.astype(F32)
            ).astype(BF)


def load_weight(place, parts, weight, sems):
    yy, xx, cc = place[1], place[2], place[3]
    copies = []
    for first in range(2):
        for other in range(2):
            half = parts[(other * 2 + first) * 4 : (other * 2 + first) * 4 + 4]
            start = (cc if other == 0 else 1 - cc) * 12 + first * 6
            for far in range(4):
                for near in range(4):
                    if first == 0:
                        yat, xat = lax.rem(yy + far, 4), lax.rem(xx + near, 4)
                    else:
                        yat, xat = lax.rem(yy + near, 4), lax.rem(xx + far, 4)
                    copies.append(
                        pltpu.make_async_copy(
                            half[far].at[near],
                            weight.at[pl.ds(start, 6), yat * 4 + xat],
                            sems.at[len(copies)],
                        )
                    )
    for copy in copies:
        copy.start()
    return copies


def head_part_kernel(place, *refs):
    g_far, parts, part, (g, weight, sums, sems, out_sems) = refs[0], refs[1:17], refs[17:28], refs[28:]
    take = pltpu.make_async_copy(g_far, g, sems.at[64])
    take.start()
    copies = load_weight(place, parts, weight, sems)
    take.wait()
    for copy in copies:
        copy.wait()
    leaving = []
    for f in (4, 3, 5, 2, 6, 1, 7, 0):
        to = lax.rem(place[0] + f, 8)
        w = weight[pl.ds(to * 3, 3)].reshape(3 * HD, weight.shape[3])
        sums[f] = dot(g[...], w, NT).astype(BF)
        if f in (3, 4, 5):
            spot = 5 + (f - 3) * 2
            pieces = [(sums.at[f, :BLK], part[spot]), (sums.at[f, BLK:], part[spot + 1])]
        else:
            spot = f if f < 3 else f - 3
            pieces = [(sums.at[f], part[spot])]
        for n, (src, dst) in enumerate(pieces):
            leaving.append(pltpu.make_async_copy(src, dst, out_sems.at[f * 2 + n]))
            leaving[-1].start()
    for copy in leaving:
        copy.wait()


def weight_grad_kernel(place, *refs):
    g_far, s_far, kept, got = refs[:4]
    out_a, out_b, (g, s, mine, theirs, made, sems, out_sems) = refs[4:8], refs[8:12], refs[12:]
    copies = [
        pltpu.make_async_copy(src, dst, sems.at[i])
        for i, (src, dst) in enumerate(((g_far, g), (s_far, s), (kept, mine), (got, theirs)))
    ]
    for copy in copies:
        copy.start()
    for copy in copies:
        copy.wait()
    leaving = []
    for k in range(4):
        w = dot(mine[k], g[...], TN) + dot(theirs[k], s[...], TN)
        made[k] = w.astype(BF).reshape(3, 4, 4, ROWS, g.shape[1])
        group = lax.rem(place[0] + k, 4)
        spot = pl.ds(lax.rem(group, 2) * 3, 3)
        along_x, along_y = [], []
        for i in range(4):
            xat, yat = lax.rem(place[2] + i, 4), lax.rem(place[1] + i, 4)
            sem = out_sems.at[k * 4 + i]
            along_x.append(pltpu.make_async_copy(made.at[k, :, :, xat], out_a[i].at[spot], sem))
            along_y.append(pltpu.make_async_copy(made.at[k, :, yat], out_b[i].at[spot], sem))

        @pl.when(group < 2)
        def start_x():
            for copy in along_x:
                copy.start()

        @pl.when(group >= 2)
        def start_y():
            for copy in along_y:
                copy.start()

        leaving += along_x
    for copy in leaving:
        copy.wait()


def middle_kernel(place, *refs):
    yy, xx = place[1], place[2]
    for ins, outs, at in ((refs[:4], refs[8:12], yy), (refs[4:8], refs[12:16], xx)):
        for k in range(4):
            to = lax.rem(at + k, 4)
            total = ins[0][:, to].astype(F32)
            for i in (1, 2, 3):
                total = total + ins[i][:, to].astype(F32)
            outs[k][...] = total.astype(BF)


def last_kernel(*refs):
    out = refs[8]
    for first in range(2):
        total = refs[first * 4][...].astype(F32)
        for i in (1, 2, 3):
            total = total + refs[first * 4 + i][...].astype(F32)
        out[first * 6 : first * 6 + 6] = total


def by_head(dims, at=0):
    return pl.BlockSpec((3, *dims), lambda h, *_: (h + at, *([0] * len(dims))))


def gridded(kernel, outs, specs, ins, place, name):
    moved = sum(math.prod(o.shape) * o.dtype.itemsize for o in outs) + sum(
        math.prod(i.shape) * i.dtype.itemsize for i in ins
    )
    return pl.pallas_call(
        kernel,
        grid_spec=pltpu.PrefetchScalarGridSpec(
            num_scalar_prefetch=1,
            grid=(2,),
            in_specs=specs,
            out_specs=[by_head(o.shape[1:]) for o in outs],
        ),
        out_shape=[pltpu.HBM(o.shape, o.dtype) for o in outs],
        compiler_params=pltpu.CompilerParams(vmem_limit_bytes=56 << 20),
        cost_estimate=pl.CostEstimate(flops=1000, bytes_accessed=moved, transcendentals=0),
        name=name,
    )(place, *ins)


def project_kernel(place, *refs):
    rel, parts, out, (held, weight, acc, sems) = refs[:8], refs[8:24], refs[25], refs[26:]
    copies = load_weight(place, parts, weight, sems)
    copies += [pltpu.make_async_copy(rel[f], held.at[f], sems.at[64 + f]) for f in range(8)]
    for copy in copies[64:]:
        copy.start()
    for copy in copies:
        copy.wait()
    for f in range(8):
        at = lax.rem(place[0] + f, 8)
        w = weight[pl.ds(at * 3, 3)].reshape(3 * HD, weight.shape[3])
        term = dot(held[f], w)
        acc[...] = term if f == 0 else acc[...] + term
    out[...] = acc[...].astype(BF)


def gather_four(v, axis):
    return [v, shift(v, axis, -1), shift(v, axis, 2), shift(v, axis, 1)]


def shards(queries, key_rows, value_rows, pattern, out_weight, out_grad):
    width = queries.shape[1]
    core = lax.axis_index("core")
    z = lax.axis_index("z")
    place = jnp.stack([z, lax.axis_index("y"), lax.axis_index("x"), core]).astype(jnp.int32)
    feats = out_weight.shape[2]

    kv = jnp.stack([key_rows.reshape(2, BLK, width), value_rows.reshape(2, BLK, width)], axis=1)
    pieces = kv.reshape(2, 32, ROWS, width).transpose(1, 0, 2, 3)
    wanted = pattern[:, 5:].reshape(1, 1, 1, 6).astype(BF)
    wanted = jnp.pad(wanted, ((0, 0), (0, 0), (0, ROWS - 1), (0, width - 6)))
    sent = jnp.concatenate([pieces, jnp.broadcast_to(wanted, (32, 1, ROWS, width))], axis=1)
    prev = shift(kv[1], SEQ, 1)
    following = shift(kv[0], SEQ, -1)
    spread = lax.all_to_all(sent, SEQ, split_axis=0, concat_axis=0, tiled=True)

    mine = lax.dynamic_slice_in_dim(out_weight, core * 12, 12, axis=1)
    theirs = shift(lax.dynamic_slice_in_dim(out_weight, 12 - core * 12, 12, axis=1), "core", 1)
    chip = jnp.where(
        core == 0, jnp.concatenate([mine, theirs], 0), jnp.concatenate([theirs, mine], 0)
    ).transpose(1, 0, 2)
    beside_grad = shift(out_grad, "core", 1)
    chip, prev, following, beside_grad = lax.optimization_barrier(
        (chip, prev, following, beside_grad)
    )
    near_a = jnp.stack(gather_four(chip[:6], "x"), 0)
    near_b = jnp.stack(gather_four(chip[6:], "y"), 0)
    own_parts = gather_four(near_a, "y") + gather_four(near_b, "x")
    ids = spread[:, 2, 0, :6].astype(jnp.int32)
    global_ids = jnp.broadcast_to(pattern[0:1, 3:5], (32, 2))
    block_of = jnp.concatenate([global_ids, ids], axis=1).reshape(256)
    picked = call(
        select_kernel,
        shape((256, ROWS, width)),
        [(block_of // 2) * 3 + block_of % 2, spread.reshape(96, ROWS, width)],
        1000,
        name="select",
        far=[near_a, near_b],
    )
    *own_parts, _ = lax.optimization_barrier((*own_parts, picked))
    parts = own_parts + [shift(p, "core", 1) for p in own_parts]
    part = call(
        head_part_kernel,
        [shape((2 * BLK, width))] * 5 + [shape((BLK, width))] * 6,
        [place],
        2 * 256 * 3072 * 768,
        [
            pltpu.VMEM((2 * BLK, feats), BF),
            pltpu.VMEM((24, 16, ROWS, feats), BF),
            pltpu.VMEM((8, 2 * BLK, width), BF),
            pltpu.SemaphoreType.DMA((65,)),
            pltpu.SemaphoreType.DMA((16,)),
        ],
        name="head_part",
        far=[out_grad, *parts],
        vmem=56,
        out=HBM,
    )

    routed = lax.all_to_all(
        picked.reshape(32, 8, ROWS, width), SEQ, split_axis=0, concat_axis=0, tiled=True
    )
    sets = [pltpu.VMEM((8 * BLK, width), BF)] * 2
    attended, probs = call(
        forward_kernel,
        [shape((2 * BLK, width)), shape((6, BLK, 8 * BLK), F32)],
        [queries, key_rows, value_rows, prev, following, routed],
        2 * 2 * 6 * 128 * 1024 * 128,
        sets,
        name="attention_forward",
        far=[part[0]],
    )

    half = BLK
    add = lambda a, b: (a.astype(F32) + b.astype(F32)).astype(BF)
    pass_on = lambda pair: (shift(pair[0], "z", 1), shift(pair[1], "z", -1))
    right, left = pass_on((part[7], part[8]))
    right = jnp.concatenate([add(part[5], right), part[6]], 0)
    left = jnp.concatenate([part[9], add(part[10], left)], 0)
    rel = {0: attended}
    ahead = behind = attended
    for k in (1, 2, 3):
        right, left = pass_on((right, left))
        if k < 3:
            right, left = add(part[3 - k], right), add(part[2 + k], left)
        ahead, behind = shift(ahead, "z", -1), shift(behind, "z", 1)
        rel[k], rel[8 - k] = ahead, behind
        right, left, ahead, behind = lax.optimization_barrier((right, left, ahead, behind))
    head_grad = (part[0].astype(F32) + right.astype(F32) + left.astype(F32)).astype(BF)
    query_grad, terms, edges, own = call(
        backward_kernel,
        [
            shape((2 * BLK, width)),
            shape((32, 8, ROWS, width)),
            shape((2, 2, BLK, width)),
            shape((2, 2, BLK, width), F32),
        ],
        [queries, key_rows, value_rows, prev, following, routed, probs, head_grad],
        5 * 2 * 6 * 128 * 1024 * 128,
        sets + [pltpu.VMEM((2, 8 * BLK, width), F32)],
        name="attention_backward",
    )
    far_a, far_b = shift(ahead[:half], "z", -1), shift(behind[half:], "z", 1)
    far_a, far_b, edges = lax.optimization_barrier((far_a, far_b, edges))
    rel[4] = jnp.concatenate([far_a, far_b], 0)
    rel = [rel[k] for k in range(8)]
    own_k = [(z + k) % 8 // 4 == core for k in range(4)]
    kept = jnp.stack([jnp.where(own_k[k], rel[k], rel[k + 4]) for k in range(4)], 0)
    given = jnp.stack([jnp.where(own_k[k], rel[k + 4], rel[k]) for k in range(4)], 0)
    got = shift(given, "core", 1)
    pair = call(
        weight_grad_kernel,
        [shape((6, 4, ROWS, feats))] * 8,
        [place],
        2 * 256 * 3072 * 768,
        [
            pltpu.VMEM((2 * BLK, feats), BF),
            pltpu.VMEM((2 * BLK, feats), BF),
            pltpu.VMEM((4, 2 * BLK, width), BF),
            pltpu.VMEM((4, 2 * BLK, width), BF),
            pltpu.VMEM((4, 3, 4, 4, ROWS, feats), BF),
            pltpu.SemaphoreType.DMA((4,)),
            pltpu.SemaphoreType.DMA((16,)),
        ],
        name="weight_grad",
        far=[out_grad, beside_grad, kept, got],
        vmem=56,
        out=HBM,
    )
    terms = lax.all_to_all(terms, SEQ, split_axis=0, concat_axis=0, tiled=True)
    after = shift(edges[0], SEQ, -1)
    before = shift(edges[1], SEQ, 1)
    sums = call(
        gather_kernel,
        shape((64, ROWS, width)),
        [block_of, terms.reshape(256, ROWS, width)],
        1000,
        [pltpu.VMEM((64, ROWS, width), F32)],
        name="gather",
    )
    projected = call(
        project_kernel,
        shape((2 * BLK, feats)),
        [place],
        2 * 256 * 3072 * 768,
        [
            pltpu.VMEM((8, 2 * BLK, width), BF),
            pltpu.VMEM((24, 16, ROWS, feats), BF),
            pltpu.VMEM((2 * BLK, feats), F32),
            pltpu.SemaphoreType.DMA((72,)),
        ],
        name="project",
        far=[*rel, *parts, sums],
        vmem=56,
    )
    back = lax.all_to_all(
        sums.reshape(32, 2, ROWS, width), SEQ, split_axis=0, concat_axis=0, tiled=True
    )
    key_grad, value_grad = call(
        final_kernel,
        [shape((2 * BLK, width)), shape((2 * BLK, width))],
        [own, back, before, after],
        1000,
        name="final",
    )

    send = lambda v, axis: [v[0]] + [shift(v[k], axis, k) for k in (1, 2, 3)]
    arrived = send(pair[:4], "x") + send(pair[4:], "y")
    *arrived, projected = lax.optimization_barrier((*arrived, projected))
    middle = gridded(
        middle_kernel,
        [shape((6, ROWS, feats))] * 8,
        [by_head((4, ROWS, feats))] * 8,
        arrived,
        place,
        "middle",
    )
    total = call(
        last_kernel,
        shape((12, ROWS, feats), F32),
        send(middle[:4], "y") + send(middle[4:], "x"),
        1000,
        name="last",
    )
    stay = lax.dynamic_slice_in_dim(total, core * 4, 4, axis=1)
    leave = lax.dynamic_slice_in_dim(total, 4 - core * 4, 4, axis=1)
    came = shift(leave.astype(BF), "core", 1).astype(F32)
    weight_grad = jnp.where(
        core == 0, jnp.concatenate([stay, came], 0), jnp.concatenate([came, stay], 0)
    ).transpose(1, 0, 2)
    return (projected, query_grad, key_grad, value_grad, weight_grad)


def solution(mesh):
    split = Mesh(mesh.devices.reshape(4, 4, 2, 8), ("y", "x", "core", "z"))
    rows, cols = ("y", "x", "core"), "z"
    return jax.shard_map(
        shards,
        mesh=split,
        in_specs=(
            P(rows, cols),
            P(rows, cols),
            P(rows, cols),
            P(rows, None),
            P(rows, None, cols),
            P(rows, cols),
        ),
        out_specs=(
            P(rows, cols),
            P(rows, cols),
            P(rows, cols),
            P(rows, cols),
            P(rows, None, cols),
        ),
        check_vma=False,
    )
```

```python
import math

import jax
import jax.numpy as jnp
from jax import lax
from jax.experimental import pallas as pl
from jax.experimental.pallas import tpu as pltpu
from jax.sharding import Mesh, PartitionSpec as P

HD = 128
BLK = 128
ROWS = 8
SEQ = ("y", "x", "core")
BF = jnp.bfloat16
F32 = jnp.float32
VMEM = pl.BlockSpec(memory_space=pltpu.VMEM)
HBM = pl.BlockSpec(memory_space=pl.ANY)
SMEM = pl.BlockSpec(memory_space=pltpu.SMEM)
NT = (((1,), (1,)), ((), ()))
TN = (((0,), (0,)), ((), ()))


def dot(a, b, dims=(((1,), (0,)), ((), ()))):
    return lax.dot_general(a, b, dims, preferred_element_type=F32)


def call(kernel, out_shape, ins, flops, scratch=(), name=None, far=(), vmem=16, out=VMEM):
    outs = out_shape if isinstance(out_shape, (tuple, list)) else [out_shape]
    moved = sum(math.prod(o.shape) * o.dtype.itemsize for o in outs) + sum(
        math.prod(i.shape) * i.dtype.itemsize for i in ins
    )
    multi = isinstance(out_shape, (tuple, list))
    return pl.pallas_call(
        kernel,
        out_shape=out_shape,
        in_specs=[SMEM if i.dtype == jnp.int32 else VMEM for i in ins]
        + [HBM] * len(far),
        out_specs=[out] * len(outs) if multi else out,
        scratch_shapes=list(scratch),
        compiler_params=pltpu.CompilerParams(vmem_limit_bytes=vmem << 20),
        cost_estimate=pl.CostEstimate(flops=flops, bytes_accessed=moved, transcendentals=0),
        name=name,
    )(*ins, *far)


def shape(dims, dtype=BF):
    return jax.ShapeDtypeStruct(dims, dtype)


def shift(value, axis, by):
    n = lax.axis_size(axis)
    return lax.ppermute(value, axis, [(i, (i + by) % n) for i in range(n)])


def select_kernel(where, pieces, *refs):
    out = refs[-1]

    def body(i, carry):
        out[i] = pieces[where[i]]
        return carry

    lax.fori_loop(0, out.shape[0], body, 0, unroll=8)


def load_sets(own, prev, following, routed, which, j, dest):
    base = which * 16
    if j == 0:
        dest[0:BLK] = prev[which]
    else:
        dest[0:BLK] = own[0:BLK]
    dest[BLK : 2 * BLK] = own[j * BLK : (j + 1) * BLK]
    if j == 0:
        dest[2 * BLK : 3 * BLK] = own[BLK : 2 * BLK]
    else:
        dest[2 * BLK : 3 * BLK] = following[which]
    for slot in range(3, 8):
        place = slot - 3 if slot < 5 else slot - 3 + 3 * j
        dest[slot * BLK : (slot + 1) * BLK] = routed[base : base + 16, place].reshape(
            BLK, dest.shape[1]
        )


def softmax_of(q, k, scale):
    s = dot(q, k, NT) * scale
    e = jnp.exp(s - jnp.max(s, axis=-1, keepdims=True))
    return e / jnp.sum(e, axis=-1, keepdims=True)


def forward_kernel(q, k, v, prev, following, routed, _p, att, kset, vset):
    scale = 1.0 / math.sqrt(HD)
    heads = q.shape[1] // HD
    for j in range(2):
        load_sets(k, prev, following, routed, 0, j, kset)
        load_sets(v, prev, following, routed, 1, j, vset)
        rows = pl.ds(j * BLK, BLK)
        for h in range(heads):
            cols = pl.ds(h * HD, HD)
            p = softmax_of(q[rows, cols], kset[:, cols], scale)
            att[rows, cols] = dot(p.astype(BF), vset[:, cols]).astype(BF)


def backward_kernel(q, k, v, prev, following, routed, grad_own, grad_right, grad_left, *refs):
    qg, terms, edges, own, kset, vset, acc = refs
    scale = 1.0 / math.sqrt(HD)
    heads = q.shape[1] // HD
    width = q.shape[1]
    for j in range(2):
        load_sets(k, prev, following, routed, 0, j, kset)
        load_sets(v, prev, following, routed, 1, j, vset)
        rows = pl.ds(j * BLK, BLK)
        for h in range(heads):
            cols = pl.ds(h * HD, HD)
            p = softmax_of(q[rows, cols], kset[:, cols], scale)
            g = grad_own[rows, cols].astype(F32) + grad_right[rows, cols].astype(F32)
            g = (g + grad_left[rows, cols].astype(F32)).astype(BF)
            pg = dot(g, vset[:, cols], NT)
            center = jnp.sum(p * pg, axis=-1, keepdims=True)
            sg = (p * (pg - center)).astype(BF)
            qg[rows, cols] = (dot(sg, kset[:, cols]) * scale).astype(BF)
            acc[0, :, cols] = dot(sg, q[rows, cols], TN) * scale
            acc[1, :, cols] = dot(p.astype(BF), g, TN)
        for which in range(2):
            t = lambda slot: acc[which, slot * BLK : (slot + 1) * BLK, :]
            cut = lambda a: a.astype(BF).reshape(16, ROWS, width)
            side = pl.ds(which * 16, 16)
            if j == 0:
                edges[0, which] = t(0).astype(BF)
                own[0, which] = t(1)
                own[1, which] = t(2)
            else:
                own[0, which] += t(0)
                own[1, which] += t(1)
                edges[1, which] = t(2).astype(BF)
            for slot in (3, 4):
                if j == 0:
                    terms[side, slot - 3] = cut(t(slot))
                else:
                    both = terms[side, slot - 3].reshape(BLK, width).astype(F32) + t(slot)
                    terms[side, slot - 3] = cut(both)
            for slot in (5, 6, 7):
                terms[side, slot - 3 + 3 * j] = cut(t(slot))


def gather_kernel(where, pieces, out, acc):
    acc[...] = jnp.zeros_like(acc)
    count = pieces.shape[0] // 8
    for slot in range(2):
        total = pieces[slot].astype(F32)
        for i in range(1, count):
            total = total + pieces[i * 8 + slot].astype(F32)
        acc[where[slot]] = total

    def body(i, carry):
        for slot in range(2, 8):
            at = where[i * 8 + slot]
            acc[at] = acc[at] + pieces[i * 8 + slot].astype(F32)
        return carry

    lax.fori_loop(0, count, body, 0, unroll=2)
    out[...] = acc[...].astype(BF)


def final_kernel(own, pieces, before, after, kg, vg):
    width = kg.shape[1]
    for which, out in ((0, kg), (1, vg)):
        for b in range(2):
            near = before[which] if b == 0 else after[which]
            far = pieces[which * 16 : which * 16 + 16, b].reshape(BLK, width)
            out[b * BLK : (b + 1) * BLK] = (
                own[b, which] + near.astype(F32) + far.astype(F32)
            ).astype(BF)


def load_weight(place, parts, weight, sems):
    yy, xx, cc = place[1], place[2], place[3]
    copies = []
    for first in range(2):
        for other in range(2):
            half = parts[(other * 2 + first) * 4 : (other * 2 + first) * 4 + 4]
            start = (cc if other == 0 else 1 - cc) * 12 + first * 6
            for far in range(4):
                for near in range(4):
                    if first == 0:
                        yat, xat = lax.rem(yy + far, 4), lax.rem(xx + near, 4)
                    else:
                        yat, xat = lax.rem(yy + near, 4), lax.rem(xx + far, 4)
                    copies.append(
                        pltpu.make_async_copy(
                            half[far].at[near],
                            weight.at[pl.ds(start, 6), yat * 4 + xat],
                            sems.at[len(copies)],
                        )
                    )
    for copy in copies:
        copy.start()
    return copies


def head_part_kernel(place, *refs):
    g_far, parts, part, (g, weight, sums, sems, out_sems) = refs[0], refs[1:17], refs[17:28], refs[28:]
    take = pltpu.make_async_copy(g_far, g, sems.at[64])
    take.start()
    copies = load_weight(place, parts, weight, sems)
    take.wait()
    for copy in copies:
        copy.wait()
    leaving = []
    for f in (4, 3, 5, 2, 6, 1, 7, 0):
        to = lax.rem(place[0] + f, 8)
        w = weight[pl.ds(to * 3, 3)].reshape(3 * HD, weight.shape[3])
        sums[f] = dot(g[...], w, NT).astype(BF)
        if f in (3, 4, 5):
            spot = 5 + (f - 3) * 2
            pieces = [(sums.at[f, :BLK], part[spot]), (sums.at[f, BLK:], part[spot + 1])]
        else:
            spot = f if f < 3 else f - 3
            pieces = [(sums.at[f], part[spot])]
        for n, (src, dst) in enumerate(pieces):
            leaving.append(pltpu.make_async_copy(src, dst, out_sems.at[f * 2 + n]))
            leaving[-1].start()
    for copy in leaving:
        copy.wait()


def weight_grad_kernel(place, *refs):
    g_far, s_far, kept, got = refs[:4]
    out_a, out_b, (g, s, mine, theirs, made, sems, out_sems) = refs[4:8], refs[8:12], refs[12:]
    copies = [
        pltpu.make_async_copy(src, dst, sems.at[i])
        for i, (src, dst) in enumerate(((g_far, g), (s_far, s), (kept, mine), (got, theirs)))
    ]
    for copy in copies:
        copy.start()
    for copy in copies:
        copy.wait()
    leaving = []
    for k in range(4):
        w = dot(mine[k], g[...], TN) + dot(theirs[k], s[...], TN)
        made[k] = w.astype(BF).reshape(3, 4, 4, ROWS, g.shape[1])
        group = lax.rem(place[0] + k, 4)
        spot = pl.ds(lax.rem(group, 2) * 3, 3)
        along_x, along_y = [], []
        for i in range(4):
            xat, yat = lax.rem(place[2] + i, 4), lax.rem(place[1] + i, 4)
            sem = out_sems.at[k * 4 + i]
            along_x.append(pltpu.make_async_copy(made.at[k, :, :, xat], out_a[i].at[spot], sem))
            along_y.append(pltpu.make_async_copy(made.at[k, :, yat], out_b[i].at[spot], sem))

        @pl.when(group < 2)
        def start_x():
            for copy in along_x:
                copy.start()

        @pl.when(group >= 2)
        def start_y():
            for copy in along_y:
                copy.start()

        leaving += along_x
    for copy in leaving:
        copy.wait()


def middle_kernel(place, *refs):
    yy, xx = place[1], place[2]
    for ins, outs, at in ((refs[:4], refs[8:12], yy), (refs[4:8], refs[12:16], xx)):
        for k in range(4):
            to = lax.rem(at + k, 4)
            total = ins[0][:, to].astype(F32)
            for i in (1, 2, 3):
                total = total + ins[i][:, to].astype(F32)
            outs[k][...] = total.astype(BF)


def last_kernel(*refs):
    out = refs[8]
    for first in range(2):
        total = refs[first * 4][...].astype(F32)
        for i in (1, 2, 3):
            total = total + refs[first * 4 + i][...].astype(F32)
        out[first * 6 : first * 6 + 6] = total


def by_head(dims, at=0):
    return pl.BlockSpec((3, *dims), lambda h, *_: (h + at, *([0] * len(dims))))


def gridded(kernel, outs, specs, ins, place, name):
    moved = sum(math.prod(o.shape) * o.dtype.itemsize for o in outs) + sum(
        math.prod(i.shape) * i.dtype.itemsize for i in ins
    )
    return pl.pallas_call(
        kernel,
        grid_spec=pltpu.PrefetchScalarGridSpec(
            num_scalar_prefetch=1,
            grid=(2,),
            in_specs=specs,
            out_specs=[by_head(o.shape[1:]) for o in outs],
        ),
        out_shape=[pltpu.HBM(o.shape, o.dtype) for o in outs],
        compiler_params=pltpu.CompilerParams(vmem_limit_bytes=56 << 20),
        cost_estimate=pl.CostEstimate(flops=1000, bytes_accessed=moved, transcendentals=0),
        name=name,
    )(place, *ins)


def project_kernel(place, *refs):
    rel, parts, out, (held, weight, acc, sems) = refs[:8], refs[8:24], refs[25], refs[26:]
    copies = load_weight(place, parts, weight, sems)
    copies += [pltpu.make_async_copy(rel[f], held.at[f], sems.at[64 + f]) for f in range(8)]
    for copy in copies[64:]:
        copy.start()
    for copy in copies:
        copy.wait()
    for f in range(8):
        at = lax.rem(place[0] + f, 8)
        w = weight[pl.ds(at * 3, 3)].reshape(3 * HD, weight.shape[3])
        term = dot(held[f], w)
        acc[...] = term if f == 0 else acc[...] + term
    out[...] = acc[...].astype(BF)


def ring_first_kernel(first_r, rest_r, rest_l, last_l, came_r, came_l, right, left):
    right[0:BLK] = (first_r[...].astype(F32) + came_r[...].astype(F32)).astype(BF)
    right[BLK:] = rest_r[...]
    left[0:BLK] = rest_l[...]
    left[BLK:] = (last_l[...].astype(F32) + came_l[...].astype(F32)).astype(BF)


def ring_kernel(part_r, part_l, came_r, came_l, right, left):
    for mine, came, out in ((part_r, came_r, right), (part_l, came_l, left)):
        out[...] = (mine[...].astype(F32) + came[...].astype(F32)).astype(BF)


def gather_four(v, axis):
    return [v, shift(v, axis, -1), shift(v, axis, 2), shift(v, axis, 1)]


def shards(queries, key_rows, value_rows, pattern, out_weight, out_grad):
    width = queries.shape[1]
    core = lax.axis_index("core")
    z = lax.axis_index("z")
    place = jnp.stack([z, lax.axis_index("y"), lax.axis_index("x"), core]).astype(jnp.int32)
    feats = out_weight.shape[2]

    kv = jnp.stack([key_rows.reshape(2, BLK, width), value_rows.reshape(2, BLK, width)], axis=1)
    pieces = kv.reshape(2, 32, ROWS, width).transpose(1, 0, 2, 3)
    wanted = pattern[:, 5:].reshape(1, 1, 1, 6).astype(BF)
    wanted = jnp.pad(wanted, ((0, 0), (0, 0), (0, ROWS - 1), (0, width - 6)))
    sent = jnp.concatenate([pieces, jnp.broadcast_to(wanted, (32, 1, ROWS, width))], axis=1)
    prev = shift(kv[1], SEQ, 1)
    following = shift(kv[0], SEQ, -1)
    spread = lax.all_to_all(sent, SEQ, split_axis=0, concat_axis=0, tiled=True)

    mine = lax.dynamic_slice_in_dim(out_weight, core * 12, 12, axis=1)
    theirs = shift(lax.dynamic_slice_in_dim(out_weight, 12 - core * 12, 12, axis=1), "core", 1)
    chip = jnp.where(
        core == 0, jnp.concatenate([mine, theirs], 0), jnp.concatenate([theirs, mine], 0)
    ).transpose(1, 0, 2)
    beside_grad = shift(out_grad, "core", 1)
    chip, prev, following, beside_grad = lax.optimization_barrier(
        (chip, prev, following, beside_grad)
    )
    near_a = jnp.stack(gather_four(chip[:6], "x"), 0)
    near_b = jnp.stack(gather_four(chip[6:], "y"), 0)
    own_parts = gather_four(near_a, "y") + gather_four(near_b, "x")
    ids = spread[:, 2, 0, :6].astype(jnp.int32)
    global_ids = jnp.broadcast_to(pattern[0:1, 3:5], (32, 2))
    block_of = jnp.concatenate([global_ids, ids], axis=1).reshape(256)
    picked = call(
        select_kernel,
        shape((256, ROWS, width)),
        [(block_of // 2) * 3 + block_of % 2, spread.reshape(96, ROWS, width)],
        1000,
        name="select",
        far=[near_a, near_b],
    )
    *own_parts, picked = lax.optimization_barrier((*own_parts, picked))
    parts = own_parts + [shift(p, "core", 1) for p in own_parts]
    part = call(
        head_part_kernel,
        [shape((2 * BLK, width))] * 5 + [shape((BLK, width))] * 6,
        [place],
        2 * 256 * 3072 * 768,
        [
            pltpu.VMEM((2 * BLK, feats), BF),
            pltpu.VMEM((24, 16, ROWS, feats), BF),
            pltpu.VMEM((8, 2 * BLK, width), BF),
            pltpu.SemaphoreType.DMA((65,)),
            pltpu.SemaphoreType.DMA((16,)),
        ],
        name="head_part",
        far=[out_grad, *parts],
        vmem=56,
        out=HBM,
    )

    routed = lax.all_to_all(
        picked.reshape(32, 8, ROWS, width), SEQ, split_axis=0, concat_axis=0, tiled=True
    )
    sets = [pltpu.VMEM((8 * BLK, width), BF)] * 2
    attended = call(
        forward_kernel,
        shape((2 * BLK, width)),
        [queries, key_rows, value_rows, prev, following, routed],
        2 * 2 * 6 * 128 * 1024 * 128,
        sets,
        name="attention_forward",
        far=[part[0]],
    )

    half = BLK
    ring_shape = [shape((2 * BLK, width))] * 2
    pass_on = lambda pair: (shift(pair[0], "z", 1), shift(pair[1], "z", -1))
    right, left = pass_on((part[7], part[8]))
    right, left = call(
        ring_first_kernel,
        ring_shape,
        [part[5], part[6], part[9], part[10], right, left],
        1000,
        name="ring_first",
    )
    rel = {0: attended}
    ahead = behind = attended
    for k in (1, 2, 3):
        right, left = pass_on((right, left))
        if k < 3:
            right, left = call(
                ring_kernel, ring_shape, [part[3 - k], part[2 + k], right, left], 1000, name="ring"
            )
        ahead, behind = shift(ahead, "z", -1), shift(behind, "z", 1)
        rel[k], rel[8 - k] = ahead, behind
        right, left, ahead, behind = lax.optimization_barrier((right, left, ahead, behind))
    query_grad, terms, edges, own = call(
        backward_kernel,
        [
            shape((2 * BLK, width)),
            shape((32, 8, ROWS, width)),
            shape((2, 2, BLK, width)),
            shape((2, 2, BLK, width), F32),
        ],
        [queries, key_rows, value_rows, prev, following, routed, part[0], right, left],
        5 * 2 * 6 * 128 * 1024 * 128,
        sets + [pltpu.VMEM((2, 8 * BLK, width), F32)],
        name="attention_backward",
    )
    far_a, far_b = shift(ahead[:half], "z", -1), shift(behind[half:], "z", 1)
    far_a, far_b, edges = lax.optimization_barrier((far_a, far_b, edges))
    rel[4] = jnp.concatenate([far_a, far_b], 0)
    rel = [rel[k] for k in range(8)]
    own_k = [(z + k) % 8 // 4 == core for k in range(4)]
    kept = jnp.stack([jnp.where(own_k[k], rel[k], rel[k + 4]) for k in range(4)], 0)
    given = jnp.stack([jnp.where(own_k[k], rel[k + 4], rel[k]) for k in range(4)], 0)
    got = shift(given, "core", 1)
    pair = call(
        weight_grad_kernel,
        [shape((6, 4, ROWS, feats))] * 8,
        [place],
        2 * 256 * 3072 * 768,
        [
            pltpu.VMEM((2 * BLK, feats), BF),
            pltpu.VMEM((2 * BLK, feats), BF),
            pltpu.VMEM((4, 2 * BLK, width), BF),
            pltpu.VMEM((4, 2 * BLK, width), BF),
            pltpu.VMEM((4, 3, 4, 4, ROWS, feats), BF),
            pltpu.SemaphoreType.DMA((4,)),
            pltpu.SemaphoreType.DMA((16,)),
        ],
        name="weight_grad",
        far=[out_grad, beside_grad, kept, got],
        vmem=56,
        out=HBM,
    )
    terms = lax.all_to_all(terms, SEQ, split_axis=0, concat_axis=0, tiled=True)
    after = shift(edges[0], SEQ, -1)
    before = shift(edges[1], SEQ, 1)
    sums = call(
        gather_kernel,
        shape((64, ROWS, width)),
        [block_of, terms.reshape(256, ROWS, width)],
        1000,
        [pltpu.VMEM((64, ROWS, width), F32)],
        name="gather",
    )
    projected = call(
        project_kernel,
        shape((2 * BLK, feats)),
        [place],
        2 * 256 * 3072 * 768,
        [
            pltpu.VMEM((8, 2 * BLK, width), BF),
            pltpu.VMEM((24, 16, ROWS, feats), BF),
            pltpu.VMEM((2 * BLK, feats), F32),
            pltpu.SemaphoreType.DMA((72,)),
        ],
        name="project",
        far=[*rel, *parts, sums],
        vmem=56,
    )
    back = lax.all_to_all(
        sums.reshape(32, 2, ROWS, width), SEQ, split_axis=0, concat_axis=0, tiled=True
    )
    key_grad, value_grad = call(
        final_kernel,
        [shape((2 * BLK, width)), shape((2 * BLK, width))],
        [own, back, before, after],
        1000,
        name="final",
    )

    send = lambda v, axis: [v[0]] + [shift(v[k], axis, k) for k in (1, 2, 3)]
    arrived = send(pair[:4], "x") + send(pair[4:], "y")
    *arrived, projected = lax.optimization_barrier((*arrived, projected))
    middle = gridded(
        middle_kernel,
        [shape((6, ROWS, feats))] * 8,
        [by_head((4, ROWS, feats))] * 8,
        arrived,
        place,
        "middle",
    )
    total = call(
        last_kernel,
        shape((12, ROWS, feats), F32),
        send(middle[:4], "y") + send(middle[4:], "x"),
        1000,
        name="last",
    )
    stay = lax.dynamic_slice_in_dim(total, core * 4, 4, axis=1)
    leave = lax.dynamic_slice_in_dim(total, 4 - core * 4, 4, axis=1)
    came = shift(leave.astype(BF), "core", 1).astype(F32)
    weight_grad = jnp.where(
        core == 0, jnp.concatenate([stay, came], 0), jnp.concatenate([came, stay], 0)
    ).transpose(1, 0, 2)
    return (projected, query_grad, key_grad, value_grad, weight_grad)


def solution(mesh):
    split = Mesh(mesh.devices.reshape(4, 4, 2, 8), ("y", "x", "core", "z"))
    rows, cols = ("y", "x", "core"), "z"
    return jax.shard_map(
        shards,
        mesh=split,
        in_specs=(
            P(rows, cols),
            P(rows, cols),
            P(rows, cols),
            P(rows, None),
            P(rows, None, cols),
            P(rows, cols),
        ),
        out_specs=(
            P(rows, cols),
            P(rows, cols),
            P(rows, cols),
            P(rows, cols),
            P(rows, None, cols),
        ),
        check_vma=False,
    )
```

```python
import math

import jax
import jax.numpy as jnp
from jax import lax
from jax.experimental import pallas as pl
from jax.experimental.pallas import tpu as pltpu
from jax.sharding import Mesh, PartitionSpec as P

HD = 128
BLK = 128
ROWS = 8
SEQ = ("y", "x", "core")
BF = jnp.bfloat16
F32 = jnp.float32
VMEM = pl.BlockSpec(memory_space=pltpu.VMEM)
HBM = pl.BlockSpec(memory_space=pl.ANY)
SMEM = pl.BlockSpec(memory_space=pltpu.SMEM)
NT = (((1,), (1,)), ((), ()))
TN = (((0,), (0,)), ((), ()))


def dot(a, b, dims=(((1,), (0,)), ((), ()))):
    return lax.dot_general(a, b, dims, preferred_element_type=F32)


def call(kernel, out_shape, ins, flops, scratch=(), name=None, far=(), vmem=16, out=VMEM):
    outs = out_shape if isinstance(out_shape, (tuple, list)) else [out_shape]
    moved = sum(math.prod(o.shape) * o.dtype.itemsize for o in outs) + sum(
        math.prod(i.shape) * i.dtype.itemsize for i in ins
    )
    multi = isinstance(out_shape, (tuple, list))
    return pl.pallas_call(
        kernel,
        out_shape=out_shape,
        in_specs=[SMEM if i.dtype == jnp.int32 else VMEM for i in ins]
        + [HBM] * len(far),
        out_specs=[out] * len(outs) if multi else out,
        scratch_shapes=list(scratch),
        compiler_params=pltpu.CompilerParams(vmem_limit_bytes=vmem << 20),
        cost_estimate=pl.CostEstimate(flops=flops, bytes_accessed=moved, transcendentals=0),
        name=name,
    )(*ins, *far)


def shape(dims, dtype=BF):
    return jax.ShapeDtypeStruct(dims, dtype)


def shift(value, axis, by):
    n = lax.axis_size(axis)
    return lax.ppermute(value, axis, [(i, (i + by) % n) for i in range(n)])


def select_kernel(where, pieces, *refs):
    out = refs[-1]

    def body(i, carry):
        out[i] = pieces[where[i]]
        return carry

    lax.fori_loop(0, out.shape[0], body, 0, unroll=8)


def load_sets(own, prev, following, routed, which, j, dest):
    base = which * 16
    if j == 0:
        dest[0:BLK] = prev[which]
    else:
        dest[0:BLK] = own[0:BLK]
    dest[BLK : 2 * BLK] = own[j * BLK : (j + 1) * BLK]
    if j == 0:
        dest[2 * BLK : 3 * BLK] = own[BLK : 2 * BLK]
    else:
        dest[2 * BLK : 3 * BLK] = following[which]
    for slot in range(3, 8):
        place = slot - 3 if slot < 5 else slot - 3 + 3 * j
        dest[slot * BLK : (slot + 1) * BLK] = routed[base : base + 16, place].reshape(
            BLK, dest.shape[1]
        )


def softmax_of(q, k, scale):
    s = dot(q, k, NT) * scale
    e = jnp.exp(s - jnp.max(s, axis=-1, keepdims=True))
    return e / jnp.sum(e, axis=-1, keepdims=True)


def forward_kernel(q, k, v, prev, following, routed, _p, att, kset, vset):
    scale = 1.0 / math.sqrt(HD)
    heads = q.shape[1] // HD
    for j in range(2):
        load_sets(k, prev, following, routed, 0, j, kset)
        load_sets(v, prev, following, routed, 1, j, vset)
        rows = pl.ds(j * BLK, BLK)
        for h in range(heads):
            cols = pl.ds(h * HD, HD)
            p = softmax_of(q[rows, cols], kset[:, cols], scale)
            att[rows, cols] = dot(p.astype(BF), vset[:, cols]).astype(BF)


def backward_kernel(q, k, v, prev, following, routed, grad_own, grad_right, grad_left, *refs):
    qg, terms, edges, own, kset, vset, acc = refs
    scale = 1.0 / math.sqrt(HD)
    heads = q.shape[1] // HD
    width = q.shape[1]
    for j in range(2):
        load_sets(k, prev, following, routed, 0, j, kset)
        load_sets(v, prev, following, routed, 1, j, vset)
        rows = pl.ds(j * BLK, BLK)
        for h in range(heads):
            cols = pl.ds(h * HD, HD)
            p = softmax_of(q[rows, cols], kset[:, cols], scale)
            g = grad_own[rows, cols].astype(F32) + grad_right[rows, cols].astype(F32)
            g = (g + grad_left[rows, cols].astype(F32)).astype(BF)
            pg = dot(g, vset[:, cols], NT)
            center = jnp.sum(p * pg, axis=-1, keepdims=True)
            sg = (p * (pg - center)).astype(BF)
            qg[rows, cols] = (dot(sg, kset[:, cols]) * scale).astype(BF)
            acc[0, :, cols] = dot(sg, q[rows, cols], TN) * scale
            acc[1, :, cols] = dot(p.astype(BF), g, TN)
        for which in range(2):
            t = lambda slot: acc[which, slot * BLK : (slot + 1) * BLK, :]
            cut = lambda a: a.astype(BF).reshape(16, ROWS, width)
            side = pl.ds(which * 16, 16)
            if j == 0:
                edges[0, which] = t(0).astype(BF)
                own[0, which] = t(1)
                own[1, which] = t(2)
            else:
                own[0, which] += t(0)
                own[1, which] += t(1)
                edges[1, which] = t(2).astype(BF)
            for slot in (3, 4):
                if j == 0:
                    terms[side, slot - 3] = cut(t(slot))
                else:
                    both = terms[side, slot - 3].reshape(BLK, width).astype(F32) + t(slot)
                    terms[side, slot - 3] = cut(both)
            for slot in (5, 6, 7):
                terms[side, slot - 3 + 3 * j] = cut(t(slot))


def gather_kernel(where, pieces, out, acc):
    acc[...] = jnp.zeros_like(acc)
    count = pieces.shape[0] // 8
    for slot in range(2):
        total = pieces[slot].astype(F32)
        for i in range(1, count):
            total = total + pieces[i * 8 + slot].astype(F32)
        acc[where[slot]] = total

    def body(i, carry):
        for slot in range(2, 8):
            at = where[i * 8 + slot]
            acc[at] = acc[at] + pieces[i * 8 + slot].astype(F32)
        return carry

    lax.fori_loop(0, count, body, 0, unroll=2)
    out[...] = acc[...].astype(BF)


def final_kernel(own, pieces, before, after, kg, vg):
    width = kg.shape[1]
    for which, out in ((0, kg), (1, vg)):
        for b in range(2):
            near = before[which] if b == 0 else after[which]
            far = pieces[which * 16 : which * 16 + 16, b].reshape(BLK, width)
            out[b * BLK : (b + 1) * BLK] = (
                own[b, which] + near.astype(F32) + far.astype(F32)
            ).astype(BF)


def load_weight(place, parts, weight, sems):
    yy, xx, cc = place[1], place[2], place[3]
    copies = []
    for first in range(2):
        for other in range(2):
            half = parts[(other * 2 + first) * 4 : (other * 2 + first) * 4 + 4]
            start = (cc if other == 0 else 1 - cc) * 12 + first * 6
            for far in range(4):
                for near in range(4):
                    if first == 0:
                        yat, xat = lax.rem(yy + far, 4), lax.rem(xx + near, 4)
                    else:
                        yat, xat = lax.rem(yy + near, 4), lax.rem(xx + far, 4)
                    copies.append(
                        pltpu.make_async_copy(
                            half[far].at[near],
                            weight.at[pl.ds(start, 6), yat * 4 + xat],
                            sems.at[len(copies)],
                        )
                    )
    for copy in copies:
        copy.start()
    return copies


def head_part_kernel(place, *refs):
    g_far, parts, part, (g, weight, sums, sems, out_sems) = refs[0], refs[1:17], refs[17:28], refs[28:]
    take = pltpu.make_async_copy(g_far, g, sems.at[64])
    take.start()
    copies = load_weight(place, parts, weight, sems)
    take.wait()
    for copy in copies:
        copy.wait()
    leaving = []
    for f in (4, 3, 5, 2, 6, 1, 7, 0):
        to = lax.rem(place[0] + f, 8)
        w = weight[pl.ds(to * 3, 3)].reshape(3 * HD, weight.shape[3])
        sums[f] = dot(g[...], w, NT).astype(BF)
        if f in (3, 4, 5):
            spot = 5 + (f - 3) * 2
            pieces = [(sums.at[f, :BLK], part[spot]), (sums.at[f, BLK:], part[spot + 1])]
        else:
            spot = f if f < 3 else f - 3
            pieces = [(sums.at[f], part[spot])]
        for n, (src, dst) in enumerate(pieces):
            leaving.append(pltpu.make_async_copy(src, dst, out_sems.at[f * 2 + n]))
            leaving[-1].start()
    for copy in leaving:
        copy.wait()


def weight_grad_kernel(place, *refs):
    g_far, s_far, kept, got = refs[:4]
    out_a, out_b, (g, s, mine, theirs, made, sems, out_sems) = refs[4:8], refs[8:12], refs[12:]
    copies = [
        pltpu.make_async_copy(src, dst, sems.at[i])
        for i, (src, dst) in enumerate(((g_far, g), (s_far, s), (kept, mine), (got, theirs)))
    ]
    for copy in copies:
        copy.start()
    for copy in copies:
        copy.wait()
    leaving = []
    for k in range(4):
        w = dot(mine[k], g[...], TN) + dot(theirs[k], s[...], TN)
        made[k] = w.astype(BF).reshape(3, 4, 4, ROWS, g.shape[1])
        group = lax.rem(place[0] + k, 4)
        spot = pl.ds(lax.rem(group, 2) * 3, 3)
        along_x, along_y = [], []
        for i in range(4):
            xat, yat = lax.rem(place[2] + i, 4), lax.rem(place[1] + i, 4)
            sem = out_sems.at[k * 4 + i]
            along_x.append(pltpu.make_async_copy(made.at[k, :, :, xat], out_a[i].at[spot], sem))
            along_y.append(pltpu.make_async_copy(made.at[k, :, yat], out_b[i].at[spot], sem))

        @pl.when(group < 2)
        def start_x():
            for copy in along_x:
                copy.start()

        @pl.when(group >= 2)
        def start_y():
            for copy in along_y:
                copy.start()

        leaving += along_x
    for copy in leaving:
        copy.wait()


def middle_kernel(place, *refs):
    yy, xx = place[1], place[2]
    for ins, outs, at in ((refs[:4], refs[8:12], yy), (refs[4:8], refs[12:16], xx)):
        for k in range(4):
            to = lax.rem(at + k, 4)
            total = ins[0][:, to].astype(F32)
            for i in (1, 2, 3):
                total = total + ins[i][:, to].astype(F32)
            outs[k][...] = total.astype(BF)


def last_kernel(place, *refs):
    stay, leave = refs[8], refs[9]
    for first in range(2):
        total = refs[first * 4][...].astype(F32)
        for i in (1, 2, 3):
            total = total + refs[first * 4 + i][...].astype(F32)
        low, high = total[:, :4], total[:, 4:]
        at = slice(first * 6, first * 6 + 6)
        stay[at] = jnp.where(place[3] == 0, low, high)
        leave[at] = jnp.where(place[3] == 0, high, low).astype(BF)


def by_head(dims, at=0):
    return pl.BlockSpec((3, *dims), lambda h, *_: (h + at, *([0] * len(dims))))


def gridded(kernel, outs, specs, ins, place, name):
    moved = sum(math.prod(o.shape) * o.dtype.itemsize for o in outs) + sum(
        math.prod(i.shape) * i.dtype.itemsize for i in ins
    )
    return pl.pallas_call(
        kernel,
        grid_spec=pltpu.PrefetchScalarGridSpec(
            num_scalar_prefetch=1,
            grid=(2,),
            in_specs=specs,
            out_specs=[by_head(o.shape[1:]) for o in outs],
        ),
        out_shape=[pltpu.HBM(o.shape, o.dtype) for o in outs],
        compiler_params=pltpu.CompilerParams(vmem_limit_bytes=56 << 20),
        cost_estimate=pl.CostEstimate(flops=1000, bytes_accessed=moved, transcendentals=0),
        name=name,
    )(place, *ins)


def project_kernel(place, *refs):
    rel, parts, out, (held, weight, acc, sems) = refs[:8], refs[8:24], refs[25], refs[26:]
    copies = load_weight(place, parts, weight, sems)
    copies += [pltpu.make_async_copy(rel[f], held.at[f], sems.at[64 + f]) for f in range(8)]
    for copy in copies[64:]:
        copy.start()
    for copy in copies:
        copy.wait()
    for f in range(8):
        at = lax.rem(place[0] + f, 8)
        w = weight[pl.ds(at * 3, 3)].reshape(3 * HD, weight.shape[3])
        term = dot(held[f], w)
        acc[...] = term if f == 0 else acc[...] + term
    out[...] = acc[...].astype(BF)


def ring_first_kernel(first_r, rest_r, rest_l, last_l, came_r, came_l, right, left):
    right[0:BLK] = (first_r[...].astype(F32) + came_r[...].astype(F32)).astype(BF)
    right[BLK:] = rest_r[...]
    left[0:BLK] = rest_l[...]
    left[BLK:] = (last_l[...].astype(F32) + came_l[...].astype(F32)).astype(BF)


def ring_kernel(part_r, part_l, came_r, came_l, right, left):
    for mine, came, out in ((part_r, came_r, right), (part_l, came_l, left)):
        out[...] = (mine[...].astype(F32) + came[...].astype(F32)).astype(BF)


def gather_four(v, axis):
    return [v, shift(v, axis, -1), shift(v, axis, 2), shift(v, axis, 1)]


def shards(queries, key_rows, value_rows, pattern, out_weight, out_grad):
    width = queries.shape[1]
    core = lax.axis_index("core")
    z = lax.axis_index("z")
    place = jnp.stack([z, lax.axis_index("y"), lax.axis_index("x"), core]).astype(jnp.int32)
    feats = out_weight.shape[2]

    kv = jnp.stack([key_rows.reshape(2, BLK, width), value_rows.reshape(2, BLK, width)], axis=1)
    pieces = kv.reshape(2, 32, ROWS, width).transpose(1, 0, 2, 3)
    wanted = pattern[:, 5:].reshape(1, 1, 1, 6).astype(BF)
    wanted = jnp.pad(wanted, ((0, 0), (0, 0), (0, ROWS - 1), (0, width - 6)))
    sent = jnp.concatenate([pieces, jnp.broadcast_to(wanted, (32, 1, ROWS, width))], axis=1)
    prev = shift(kv[1], SEQ, 1)
    following = shift(kv[0], SEQ, -1)
    spread = lax.all_to_all(sent, SEQ, split_axis=0, concat_axis=0, tiled=True)

    mine = lax.dynamic_slice_in_dim(out_weight, core * 12, 12, axis=1)
    theirs = shift(lax.dynamic_slice_in_dim(out_weight, 12 - core * 12, 12, axis=1), "core", 1)
    chip = jnp.where(
        core == 0, jnp.concatenate([mine, theirs], 0), jnp.concatenate([theirs, mine], 0)
    ).transpose(1, 0, 2)
    beside_grad = shift(out_grad, "core", 1)
    chip, prev, following, beside_grad = lax.optimization_barrier(
        (chip, prev, following, beside_grad)
    )
    near_a = jnp.stack(gather_four(chip[:6], "x"), 0)
    near_b = jnp.stack(gather_four(chip[6:], "y"), 0)
    own_parts = gather_four(near_a, "y") + gather_four(near_b, "x")
    ids = spread[:, 2, 0, :6].astype(jnp.int32)
    global_ids = jnp.broadcast_to(pattern[0:1, 3:5], (32, 2))
    block_of = jnp.concatenate([global_ids, ids], axis=1).reshape(256)
    picked = call(
        select_kernel,
        shape((256, ROWS, width)),
        [(block_of // 2) * 3 + block_of % 2, spread.reshape(96, ROWS, width)],
        1000,
        name="select",
        far=[near_a, near_b],
    )
    *own_parts, picked = lax.optimization_barrier((*own_parts, picked))
    parts = own_parts + [shift(p, "core", 1) for p in own_parts]
    part = call(
        head_part_kernel,
        [shape((2 * BLK, width))] * 5 + [shape((BLK, width))] * 6,
        [place],
        2 * 256 * 3072 * 768,
        [
            pltpu.VMEM((2 * BLK, feats), BF),
            pltpu.VMEM((24, 16, ROWS, feats), BF),
            pltpu.VMEM((8, 2 * BLK, width), BF),
            pltpu.SemaphoreType.DMA((65,)),
            pltpu.SemaphoreType.DMA((16,)),
        ],
        name="head_part",
        far=[out_grad, *parts],
        vmem=56,
        out=HBM,
    )

    routed = lax.all_to_all(
        picked.reshape(32, 8, ROWS, width), SEQ, split_axis=0, concat_axis=0, tiled=True
    )
    sets = [pltpu.VMEM((8 * BLK, width), BF)] * 2
    attended = call(
        forward_kernel,
        shape((2 * BLK, width)),
        [queries, key_rows, value_rows, prev, following, routed],
        2 * 2 * 6 * 128 * 1024 * 128,
        sets,
        name="attention_forward",
        far=[part[0]],
    )

    half = BLK
    ring_shape = [shape((2 * BLK, width))] * 2
    pass_on = lambda pair: (shift(pair[0], "z", 1), shift(pair[1], "z", -1))
    right, left = pass_on((part[7], part[8]))
    right, left = call(
        ring_first_kernel,
        ring_shape,
        [part[5], part[6], part[9], part[10], right, left],
        1000,
        name="ring_first",
    )
    rel = {0: attended}
    ahead = behind = attended
    for k in (1, 2, 3):
        right, left = pass_on((right, left))
        if k < 3:
            right, left = call(
                ring_kernel, ring_shape, [part[3 - k], part[2 + k], right, left], 1000, name="ring"
            )
        ahead, behind = shift(ahead, "z", -1), shift(behind, "z", 1)
        rel[k], rel[8 - k] = ahead, behind
        right, left, ahead, behind = lax.optimization_barrier((right, left, ahead, behind))
    query_grad, terms, edges, own = call(
        backward_kernel,
        [
            shape((2 * BLK, width)),
            shape((32, 8, ROWS, width)),
            shape((2, 2, BLK, width)),
            shape((2, 2, BLK, width), F32),
        ],
        [queries, key_rows, value_rows, prev, following, routed, part[0], right, left],
        5 * 2 * 6 * 128 * 1024 * 128,
        sets + [pltpu.VMEM((2, 8 * BLK, width), F32)],
        name="attention_backward",
    )
    far_a, far_b = shift(ahead[:half], "z", -1), shift(behind[half:], "z", 1)
    far_a, far_b, edges = lax.optimization_barrier((far_a, far_b, edges))
    rel[4] = jnp.concatenate([far_a, far_b], 0)
    rel = [rel[k] for k in range(8)]
    own_k = [(z + k) % 8 // 4 == core for k in range(4)]
    kept = jnp.stack([jnp.where(own_k[k], rel[k], rel[k + 4]) for k in range(4)], 0)
    given = jnp.stack([jnp.where(own_k[k], rel[k + 4], rel[k]) for k in range(4)], 0)
    got = shift(given, "core", 1)
    pair = call(
        weight_grad_kernel,
        [shape((6, 4, ROWS, feats))] * 8,
        [place],
        2 * 256 * 3072 * 768,
        [
            pltpu.VMEM((2 * BLK, feats), BF),
            pltpu.VMEM((2 * BLK, feats), BF),
            pltpu.VMEM((4, 2 * BLK, width), BF),
            pltpu.VMEM((4, 2 * BLK, width), BF),
            pltpu.VMEM((4, 3, 4, 4, ROWS, feats), BF),
            pltpu.SemaphoreType.DMA((4,)),
            pltpu.SemaphoreType.DMA((16,)),
        ],
        name="weight_grad",
        far=[out_grad, beside_grad, kept, got],
        vmem=56,
        out=HBM,
    )
    terms = lax.all_to_all(terms, SEQ, split_axis=0, concat_axis=0, tiled=True)
    after = shift(edges[0], SEQ, -1)
    before = shift(edges[1], SEQ, 1)
    sums = call(
        gather_kernel,
        shape((64, ROWS, width)),
        [block_of, terms.reshape(256, ROWS, width)],
        1000,
        [pltpu.VMEM((64, ROWS, width), F32)],
        name="gather",
    )
    projected = call(
        project_kernel,
        shape((2 * BLK, feats)),
        [place],
        2 * 256 * 3072 * 768,
        [
            pltpu.VMEM((8, 2 * BLK, width), BF),
            pltpu.VMEM((24, 16, ROWS, feats), BF),
            pltpu.VMEM((2 * BLK, feats), F32),
            pltpu.SemaphoreType.DMA((72,)),
        ],
        name="project",
        far=[*rel, *parts, sums],
        vmem=56,
    )
    back = lax.all_to_all(
        sums.reshape(32, 2, ROWS, width), SEQ, split_axis=0, concat_axis=0, tiled=True
    )
    key_grad, value_grad = call(
        final_kernel,
        [shape((2 * BLK, width)), shape((2 * BLK, width))],
        [own, back, before, after],
        1000,
        name="final",
    )

    send = lambda v, axis: [v[0]] + [shift(v[k], axis, k) for k in (1, 2, 3)]
    arrived = send(pair[:4], "x") + send(pair[4:], "y")
    *arrived, projected = lax.optimization_barrier((*arrived, projected))
    middle = gridded(
        middle_kernel,
        [shape((6, ROWS, feats))] * 8,
        [by_head((4, ROWS, feats))] * 8,
        arrived,
        place,
        "middle",
    )
    stay, leave = call(
        last_kernel,
        [shape((12, 4, feats), F32), shape((12, 4, feats))],
        [place, *send(middle[:4], "y"), *send(middle[4:], "x")],
        1000,
        name="last",
    )
    came = shift(leave, "core", 1).astype(F32)
    weight_grad = jnp.where(
        core == 0, jnp.concatenate([stay, came], 0), jnp.concatenate([came, stay], 0)
    ).transpose(1, 0, 2)
    return (projected, query_grad, key_grad, value_grad, weight_grad)


def solution(mesh):
    split = Mesh(mesh.devices.reshape(4, 4, 2, 8), ("y", "x", "core", "z"))
    rows, cols = ("y", "x", "core"), "z"
    return jax.shard_map(
        shards,
        mesh=split,
        in_specs=(
            P(rows, cols),
            P(rows, cols),
            P(rows, cols),
            P(rows, None),
            P(rows, None, cols),
            P(rows, cols),
        ),
        out_specs=(
            P(rows, cols),
            P(rows, cols),
            P(rows, cols),
            P(rows, cols),
            P(rows, None, cols),
        ),
        check_vma=False,
    )
```
